32 devices in a mesh: scen: 2 (over x), row: 4 (over y, core), col: 4 (over z).
Axes of the slice: x: 2, y: 2, z: 4, core: 2. Of those that a mesh axis runs over, the one named last changes fastest.
Arguments:
- root_matrix: float32 [8192, 8192], P(('scen', 'row'), 'col'), may hold values from -1 to 32, as said below
- inverse_block: bfloat16 [32, 1024, 1024], P(('scen', 'row', 'col')), may hold values from -0.05 to 3, as said below
- link_tiles: bfloat16 [32, 20, 1024, 128], P(('scen', 'row', 'col')), may hold values from -0.1875 to 0.1875
- tile_mask: int32 [32, 64], P(('scen', 'row', 'col')), may hold values from 0 to 1, as said below
- panel_index: int32 [1], replicated, may hold values from 0 to 31
Outputs:
- trailing: float32 [8192, 8192], P(('scen', 'row'), 'col')
- factor: float32 [8192, 128], P(('scen', 'row', 'col'))
The draws below stay inside these ranges and needn't reach their ends.
Inputs may be any that keep to these rules, and one draw needn't show every extreme that they name: `root_matrix`: Symmetric, with the diagonal between 8 and 32 and every other entry of magnitude under 1. `inverse_block`: each block is symmetric positive definite, its diagonal between 1 and 3. `tile_mask`: each scenario flags between 4 and 20 tiles, at most 4 among each aligned group of 8 tiles (tiles 0 to 7, and so on); some scenario flags exactly 20 tiles, 4 in each of its first groups.
All inputs are finite; a program needn't handle non-finite values.
Results may differ from the reference program's by a relative error of at most 0.00049.
Values may be sent and summed in bfloat16 or wider, within the bound.
A program may use at most 64 MiB of HBM per device.

```python
import math
import jax
import jax.numpy as jnp
from jax import lax

NS = 1024
NF = 8192
PANEL = 128
TILE = 128
MAXT = 20
TGROUP = 8
TCAP = 4
NT = 64
SCENS = 32


def draw_root_matrix(key, part):
    noise_key, diag_key = jax.random.split(jax.random.fold_in(key, 11))
    noise_part = jnp.clip(0.1 * jax.random.normal(noise_key, (NF, NF), jnp.float32), -0.6, 0.6)
    symmetric = (noise_part + noise_part.T) * 0.7071
    diag_vals = jnp.exp(jax.random.uniform(diag_key, (NF,), jnp.float32, math.log(8.0), math.log(32.0)))
    row_ids = lax.broadcasted_iota(jnp.int32, (NF, NF), 0)
    col_ids = lax.broadcasted_iota(jnp.int32, (NF, NF), 1)
    return jnp.where(row_ids == col_ids, diag_vals[:, None], symmetric)


def one_inverse(scen_key):
    noise_key, diag_key = jax.random.split(scen_key)
    noise_part = jnp.clip(0.01 * jax.random.normal(noise_key, (NS, NS), jnp.float32), -0.035, 0.035)
    symmetric = (noise_part + noise_part.T) * 0.7071
    diag_vals = jnp.exp(jax.random.uniform(diag_key, (NS,), jnp.float32, 0.0, math.log(3.0)))
    row_ids = lax.broadcasted_iota(jnp.int32, (NS, NS), 0)
    col_ids = lax.broadcasted_iota(jnp.int32, (NS, NS), 1)
    return jnp.where(row_ids == col_ids, diag_vals[:, None], symmetric).astype(jnp.bfloat16)


def draw_inverse_block(key, part):
    scen_keys = jax.random.split(jax.random.fold_in(key, 13), SCENS)
    return lax.map(one_inverse, scen_keys)


def group_ranks(group_key):
    return jnp.argsort(jax.random.permutation(group_key, TGROUP))


def one_mask(scen_key, count, forced_here):
    slot_key, tile_key = jax.random.split(scen_key)
    group_count = NT // TGROUP
    slot_total = group_count * TCAP
    slot_pos = jnp.argsort(jax.random.permutation(slot_key, slot_total))
    slot_pos = jnp.where(forced_here, jnp.arange(slot_total), slot_pos)
    chosen = (slot_pos < count).astype(jnp.int32)
    per_group = jnp.sum(chosen.reshape(group_count, TCAP), axis=1)
    ranks = jax.vmap(group_ranks)(jax.random.split(tile_key, group_count))
    return (ranks < per_group[:, None]).astype(jnp.int32).reshape(NT)


def draw_tile_mask(key, part):
    count_key, order_key, full_key = jax.random.split(jax.random.fold_in(key, 17), 3)
    counts = jax.random.randint(count_key, (SCENS,), 4, MAXT + 1)
    forced = jax.random.randint(full_key, (), 0, SCENS)
    forced_flags = jnp.arange(SCENS) == forced
    counts = jnp.where(forced_flags, MAXT, counts)
    return jax.vmap(one_mask)(jax.random.split(order_key, SCENS), counts, forced_flags)


def shard_levels(rng, dims, pieces, least, high):
    level, own = 1.0, jax.random.fold_in(rng, 6)
    for dim, shards_of in pieces:
        heights = jnp.exp(jax.random.uniform(jax.random.fold_in(own, dim), (shards_of,), jnp.float32, least / len(pieces), high / len(pieces)))
        level = level * jnp.repeat(heights, dims[dim] // shards_of).reshape([-1 if axis == dim else 1 for axis in range(len(dims))])
    return level


def gaussian(own_key, shape, width, reach, pieces=(), held_as=jnp.bfloat16):
    entries = width * jax.random.normal(own_key, shape, jnp.float32)
    if pieces:
        entries = entries * shard_levels(own_key, shape, pieces, -0.22, 0.18)
    return jnp.clip(entries, -reach, reach).astype(held_as)


def setup_inputs(seed: int = 0) -> dict:
    key_list = jax.random.split(jax.random.key(seed), 6)
    return {
        "root_matrix": draw_root_matrix(jax.random.fold_in(key_list[5], 71), 0),
        "inverse_block": draw_inverse_block(jax.random.fold_in(key_list[5], 71), 0),
        "link_tiles": gaussian(key_list[2], (SCENS, MAXT, NS, TILE), NS ** -0.5, 0.1875, ((0, 32),)),
        "tile_mask": draw_tile_mask(jax.random.fold_in(key_list[5], 71), 0),
        "panel_index": jax.random.randint(key_list[4], (1,), 0, NF // (2 * PANEL)).astype(jnp.int32),
    }


def select_matrix(tile_flags, slot_count):
    slot_order = jnp.cumsum(tile_flags) - 1
    slot_ids = lax.broadcasted_iota(jnp.int32, (slot_count, tile_flags.shape[0]), 0)
    hit = (slot_order[None, :] == slot_ids) & (tile_flags[None, :] == 1)
    return jnp.where(hit, jnp.float32(1.0), jnp.float32(0.0))

def scenario_term(inverse, tiles_here, tile_flags, panel_at):
    slot_count, inner_rows, tile_rows = tiles_here.shape
    selector = select_matrix(tile_flags, slot_count)
    per_panel = PANEL // tile_rows
    picked = lax.dynamic_slice_in_dim(selector, panel_at * per_panel, per_panel, 1)
    columns = jnp.einsum('kj,knt->njt', picked, tiles_here.astype(jnp.float32), precision=lax.Precision.HIGHEST)
    columns = columns.reshape(inner_rows, PANEL).astype(jnp.bfloat16)
    weighted = jnp.dot(inverse.astype(jnp.float32), columns.astype(jnp.float32), preferred_element_type=jnp.float32).astype(jnp.bfloat16)
    product = jnp.einsum('knt,na->kta', tiles_here.astype(jnp.float32), weighted.astype(jnp.float32), precision=lax.Precision.HIGHEST)
    spread = jnp.einsum('kr,kta->rta', selector, product, precision=lax.Precision.HIGHEST)
    return spread.reshape(selector.shape[1] * tile_rows, PANEL)

def reference(root_matrix, inverse_block, link_tiles, tile_mask, panel_index):
    panel_at = panel_index[0]
    first_col = panel_at * PANEL
    base_cols = lax.dynamic_slice_in_dim(root_matrix, first_col, PANEL, 1)

    def accumulate(running, scenario_items):
        inverse, tiles_here, tile_flags = scenario_items
        return (running + scenario_term(inverse, tiles_here, tile_flags, panel_at), None)
    panel_sum, _ = lax.scan(accumulate, base_cols, (inverse_block, link_tiles, tile_mask))
    diagonal = lax.dynamic_slice_in_dim(panel_sum, first_col, PANEL, 0)
    chol_lower = jnp.linalg.cholesky(diagonal)
    solved = jax.scipy.linalg.solve_triangular(chol_lower, panel_sum.T, lower=True).T
    row_ids = lax.broadcasted_iota(jnp.int32, (NF, 1), 0)
    factor = jnp.where(row_ids >= first_col, solved, jnp.zeros_like(solved))
    rounded = factor.astype(jnp.bfloat16)
    ending = jnp.where(row_ids >= first_col + PANEL, rounded, jnp.zeros_like(rounded))
    update = jnp.dot(ending.astype(jnp.float32), ending.T.astype(jnp.float32), preferred_element_type=jnp.float32)
    return (root_matrix - update, factor)
```

```python
import jax
import jax.numpy as jnp
from jax import lax
from jax.experimental import pallas as pl
from jax.experimental.pallas import tpu as pltpu
from jax.sharding import PartitionSpec as P

PANEL = 128


def broadcast(block, axis, source):
    block = jnp.where(lax.axis_index(axis) == source, block, jnp.zeros_like(block))
    return lax.psum(block, axis)


def select_matrix(tile_flags, slot_count):
    slot_order = jnp.cumsum(tile_flags) - 1
    slot_ids = lax.broadcasted_iota(jnp.int32, (slot_count, tile_flags.shape[0]), 0)
    hit = (slot_order[None, :] == slot_ids) & (tile_flags[None, :] == 1)
    return jnp.where(hit, jnp.float32(1.0), jnp.float32(0.0))


def compact_term(inverse, tiles_here, tile_flags, panel_at):
    slot_count, inner_rows, tile_rows = tiles_here.shape
    selector = select_matrix(tile_flags, slot_count)
    per_panel = PANEL // tile_rows
    picked = lax.dynamic_slice_in_dim(selector, panel_at * per_panel, per_panel, 1)
    columns = jnp.einsum(
        "kj,knt->njt", picked.astype(jnp.bfloat16), tiles_here, preferred_element_type=jnp.float32
    )
    columns = columns.reshape(inner_rows, PANEL).astype(jnp.bfloat16)
    weighted = jnp.dot(inverse, columns, preferred_element_type=jnp.float32).astype(jnp.bfloat16)
    product = jnp.einsum("knt,na->kta", tiles_here, weighted, preferred_element_type=jnp.float32)
    return (selector, product)


def dense_term(selector, product, base_cols, base_start):
    spread = jnp.einsum("kr,kta->rta", selector, product, precision=lax.Precision.HIGHEST)
    scenario = spread.reshape(selector.shape[1] * product.shape[1], PANEL)
    own_block = lax.dynamic_slice_in_dim(scenario, base_start, base_cols.shape[0], 0) + base_cols
    return lax.dynamic_update_slice_in_dim(scenario, own_block, base_start, 0)


def lower_rows(diagonal, rows_here, first_row, first_col):
    chol_lower = jnp.linalg.cholesky(diagonal)
    solved = jax.scipy.linalg.solve_triangular(chol_lower, rows_here.T, lower=True).T
    row_ids = first_row + lax.broadcasted_iota(jnp.int32, (rows_here.shape[0], 1), 0)
    return jnp.where(row_ids >= first_col, solved, 0.0)


def trailing_rows(factor_part, first_row, first_col):
    rounded = factor_part.astype(jnp.bfloat16)
    row_ids = first_row + lax.broadcasted_iota(jnp.int32, (factor_part.shape[0], 1), 0)
    return jnp.where(row_ids >= first_col + PANEL, rounded, jnp.zeros_like(rounded))


def local(root_matrix, inverse_block, link_tiles, tile_mask, panel_index):
    panel_at = panel_index[0]
    tile_flags = tile_mask[0]
    selector, product = compact_term(inverse_block[0], link_tiles[0], tile_flags, panel_at)
    tile_count = selector.shape[1]
    tile_rows = product.shape[1]
    total_rows = tile_count * tile_rows
    row_block, col_block = root_matrix.shape
    scen_at = lax.axis_index("scen")
    row_at = lax.axis_index("row")
    col_at = lax.axis_index("col")
    row_count = lax.axis_size("row")
    col_count = lax.axis_size("col")
    scen_count = lax.axis_size("scen")
    block_at = scen_at * row_count + row_at
    first_col = panel_at * PANEL
    owner_col = first_col // col_block
    base_cols = lax.dynamic_slice_in_dim(root_matrix, first_col - owner_col * col_block, PANEL, 1)
    base_cols = jnp.where(col_at == owner_col, base_cols, 0.0)
    piece_rows = row_block // col_count
    scenario = dense_term(selector, product, base_cols, block_at * row_block)
    slab_rows = total_rows // scen_count
    slab_sum = lax.psum_scatter(scenario, "scen", scatter_dimension=0, tiled=True)
    slab_sum = lax.psum(slab_sum, ("row", "col"))
    owner_slab = first_col // slab_rows
    diag_part = lax.dynamic_slice_in_dim(slab_sum, first_col - owner_slab * slab_rows, PANEL, 0)
    diagonal = broadcast(diag_part, "scen", owner_slab)
    slab_first = scen_at * slab_rows
    slab_factor = lower_rows(diagonal, slab_sum, slab_first, first_col)
    factor_rows = lax.dynamic_slice_in_dim(
        slab_factor, (row_at * col_count + col_at) * piece_rows, piece_rows, 0
    )
    ending = trailing_rows(slab_factor, slab_first, first_col)
    all_factor = lax.all_gather(ending, "scen", axis=0, tiled=True)
    own_rows = lax.dynamic_slice_in_dim(all_factor, block_at * row_block, row_block, 0)
    own_cols = lax.dynamic_slice_in_dim(all_factor, col_at * col_block, col_block, 0)
    update = lax.dot_general(
        own_rows, own_cols, (((1,), (1,)), ((), ())), preferred_element_type=jnp.float32
    )
    return (root_matrix - update, factor_rows)


MESH_ID = pl.DeviceIdType.MESH
F32 = jnp.float32
BF16 = jnp.bfloat16


def term_kernel(panel_ref, mask_ref, inv_hbm, tiles_hbm, root_ref, out_ref, diag_ref, inv, tiles, left, sems):
    slots = tiles.shape[0]
    f = panel_ref[0]
    scen_at, row_at, col_at = (lax.axis_index(a) for a in ("scen", "row", "col"))
    group = scen_at * lax.axis_size("row") + row_at
    inv_copy = pltpu.make_async_copy(inv_hbm, inv, sems.at[slots])
    inv_copy.start()

    def tile_copy(k):
        return pltpu.make_async_copy(tiles_hbm.at[k], tiles.at[k], sems.at[k])

    tile_total = mask_ref.shape[1]
    before = lax.fori_loop(0, f, lambda t, n: n + mask_ref[0, t], 0)
    total = lax.fori_loop(f, tile_total, lambda t, n: n + mask_ref[0, t], before)
    linked = mask_ref[0, f]
    first = jnp.minimum(before, slots - 1)
    panel_copy = pltpu.make_async_copy(tiles_hbm.at[first], left, sems.at[slots + 1])
    panel_copy.start()

    @pl.loop(0, total)
    def _(k):
        tile_copy(k).start()

    panel_copy.wait()
    columns = jnp.where(linked == 1, left[...], jnp.zeros_like(left))
    inv_copy.wait()
    weighted = lax.dot_general(
        columns, inv[...], (((0,), (0,)), ((), ())), preferred_element_type=F32
    ).astype(BF16)

    def one(t, at):
        flag = mask_ref[0, t]

        @pl.when(flag == 1)
        def _():
            tile_copy(at).wait()
            out_ref[t] = jnp.dot(weighted, tiles[at], preferred_element_type=F32)

        @pl.when(flag != 1)
        def _():
            out_ref[t] = jnp.zeros(out_ref.shape[1:], F32)

        return at + flag

    lax.fori_loop(0, tile_total, one, 0)
    own_tiles = root_ref.shape[0] // PANEL

    @pl.when(col_at == f // (tile_total // lax.axis_size("col")))
    def _():
        for i in range(own_tiles):
            at = group * own_tiles + i
            out_ref[at] = out_ref[at] + root_ref[i * PANEL : (i + 1) * PANEL, :].T

    diag_ref[...] = out_ref[f]


def scenario_tiles(root_matrix, inverse, tiles, tile_mask, panel_index):
    slots, inner, tile_rows = tiles.shape
    tile_total = tile_mask.shape[1]
    own_rows, own_cols = root_matrix.shape
    wide = own_cols // PANEL
    return pl.pallas_call(
        term_kernel,
        out_shape=(
            jax.ShapeDtypeStruct((tile_total, PANEL, tile_rows), F32),
            jax.ShapeDtypeStruct((PANEL, PANEL), F32),
        ),
        grid_spec=pltpu.PrefetchScalarGridSpec(
            num_scalar_prefetch=2,
            grid=(1,),
            in_specs=[
                pl.BlockSpec(memory_space=pl.ANY),
                pl.BlockSpec(memory_space=pl.ANY),
                pl.BlockSpec((own_rows, PANEL), lambda i, p, m: (0, lax.rem(p[0], wide))),
            ],
            out_specs=[
                pl.BlockSpec((tile_total, PANEL, tile_rows), lambda i, p, m: (0, 0, 0)),
                pl.BlockSpec((PANEL, PANEL), lambda i, p, m: (0, 0)),
            ],
            scratch_shapes=[
                pltpu.VMEM(inverse.shape, BF16),
                pltpu.VMEM(tiles.shape, BF16),
                pltpu.VMEM((inner, tile_rows), BF16),
                pltpu.SemaphoreType.DMA((slots + 2,)),
            ],
        ),
        compiler_params=pltpu.CompilerParams(vmem_limit_bytes=40 * 2**20),
        name="scenario_tiles",
    )(panel_index, tile_mask, inverse, tiles, root_matrix)


def remote(src, dst, send, recv, device):
    return pltpu.make_async_remote_copy(
        src_ref=src, dst_ref=dst, send_sem=send, recv_sem=recv, device_id=device, device_id_type=MESH_ID
    )


def sum_kernel(tiles_hbm, diag_in, piece_ref, diag_ref, own, got0, got1, got2, acc, got3, got4,
               dsum, dgot, dpart, dparts, send, recv, local_sem, dsend, drecv):
    s, r, c = (lax.axis_index(a) for a in ("scen", "row", "col"))
    y, k = r // 2, lax.rem(r, 2)
    core = (s, 2 * y + 1 - k, c)
    x_to = (1 - s, r, c)
    y_to = (s, 2 * (1 - y) + k, c)
    z1 = c + 1 - 2 * lax.rem(c, 2)
    z2 = lax.rem(c + 2, 4)
    me = s * 8 + y * 4 + c

    def chip(o):
        q = lax.rem(me + o, 16)
        return q, (q // 8, 2 * lax.rem(q // 4, 2) + k, lax.rem(q, 4))

    barrier = pltpu.get_barrier_semaphore()
    pl.semaphore_signal(barrier, inc=1, device_id=core, device_id_type=MESH_ID)
    for o in range(1, 16):
        pl.semaphore_signal(barrier, inc=1, device_id=chip(o)[1], device_id_type=MESH_ID)
    pl.semaphore_wait(barrier, 16)

    core_diag = remote(diag_in, dgot, dsend.at[0], drecv.at[0], core)
    core_diag.start()
    core_copy = []
    loads = []
    for sp in range(2):
        for yp in range(2):
            i = sp * 2 + yp
            cp = remote(tiles_hbm.at[pl.ds((i * 2 + 1 - k) * 8, 8)], got0.at[i], send.at[i], recv.at[i], core)
            cp.start()
            core_copy.append(cp)
            ld = pltpu.make_async_copy(tiles_hbm.at[pl.ds((i * 2 + k) * 8, 8)], own.at[i], local_sem.at[i])
            ld.start()
            loads.append(ld)
    core_diag.wait()
    dsum[...] = diag_in[...] + dgot[...]
    out1 = []
    for o in range(1, 16):
        q, dev = chip(o)
        cp = remote(dsum.at[pl.ds(pl.multiple_of(q * 8, 8), 8)], dparts.at[o], dsend.at[o], drecv.at[o], dev)
        cp.start()
        out1.append(cp)
    for i in range(4):
        loads[i].wait()
        core_copy[i].wait()
        own[i] = own[i] + got0[i]
    order = []
    ax = []
    for step in range(2):
        yy = (1 - y) if step == 0 else y
        ss = (1 - s) if step == 0 else s
        a = remote(own.at[(1 - s) * 2 + yy, pl.ds(0, 4)], got1.at[0, step], send.at[4 + step], recv.at[4 + step], x_to)
        b = remote(own.at[ss * 2 + 1 - y, pl.ds(4, 4)], got1.at[1, step], send.at[6 + step], recv.at[6 + step], y_to)
        a.start()
        b.start()
        ax.append((a, b))
    for cp in out1:
        cp.wait_recv()
    total = dsum[pl.ds(pl.multiple_of(me * 8, 8), 8), :]
    for o in range(1, 16):
        total = total + dparts[o]
    dpart[...] = total
    diag_ref[pl.ds(pl.multiple_of(me * 8, 8), 8), :] = total
    out2 = []
    for o in range(1, 16):
        q, dev = chip(o)
        cp = remote(dpart, diag_ref.at[pl.ds(pl.multiple_of(me * 8, 8), 8)], dsend.at[15 + o], drecv.at[15 + o], dev)
        cp.start()
        out2.append(cp)
    ax[0][0].wait_recv()
    acc[0, 0] = own[s * 2 + 1 - y, 0:4] + got1[0, 0]
    a2 = remote(acc.at[0, 0], got2.at[0], send.at[8], recv.at[8], y_to)
    a2.start()
    ax[0][1].wait_recv()
    acc[0, 1] = own[(1 - s) * 2 + y, 4:8] + got1[1, 0]
    b2 = remote(acc.at[0, 1], got2.at[1], send.at[9], recv.at[9], x_to)
    b2.start()
    ax[1][0].wait_recv()
    acc[1, 0] = own[s * 2 + y, 0:4] + got1[0, 1]
    ax[1][1].wait_recv()
    acc[1, 1] = own[s * 2 + y, 4:8] + got1[1, 1]
    a2.wait_recv()
    acc[1, 0] = acc[1, 0] + got2[0]
    b2.wait_recv()
    acc[1, 1] = acc[1, 1] + got2[1]
    par = lax.rem(c, 2)
    hi = c // 2
    z_out = []
    for h in range(2):
        cp = remote(acc.at[1, h, pl.ds((1 - par) * 2, 2)], got3.at[h], send.at[10 + h], recv.at[10 + h], (s, r, z1))
        cp.start()
        z_out.append(cp)
    z_out[0].wait_recv()
    z_out[1].wait_recv()
    a2.wait_send()
    acc[0, 0, pl.ds(0, 2)] = acc[1, 1 - hi, pl.ds(par * 2, 2)] + got3[1 - hi]
    last = remote(acc.at[0, 0, pl.ds(0, 2)], got4, send.at[12], recv.at[12], (s, r, z2))
    last.start()
    mine = acc[1, hi, pl.ds(par * 2, 2)] + got3[hi]
    last.wait_recv()
    piece_ref[...] = mine + got4[...]
    for cp in out2:
        cp.wait_recv()
    for cp in out1 + out2 + [ax[0][0], ax[0][1], ax[1][0], ax[1][1], b2, *z_out, last]:
        cp.wait_send()


def reduced(tiles, diag):
    tile = tiles.shape[1:]
    vmem = pl.BlockSpec(memory_space=pltpu.VMEM)
    return pl.pallas_call(
        sum_kernel,
        out_shape=(jax.ShapeDtypeStruct((2, *tile), F32), jax.ShapeDtypeStruct((PANEL, PANEL), F32)),
        in_specs=[pl.BlockSpec(memory_space=pl.ANY), vmem],
        out_specs=(vmem, vmem),
        scratch_shapes=[
            pltpu.VMEM((4, 8, *tile), F32),
            pltpu.VMEM((4, 8, *tile), F32),
            pltpu.VMEM((2, 2, 4, *tile), F32),
            pltpu.VMEM((2, 4, *tile), F32),
            pltpu.VMEM((2, 2, 4, *tile), F32),
            pltpu.VMEM((2, 2, *tile), F32),
            pltpu.VMEM((2, *tile), F32),
            pltpu.VMEM(tile, F32),
            pltpu.VMEM(tile, F32),
            pltpu.VMEM((8, PANEL), F32),
            pltpu.VMEM((16, 8, PANEL), F32),
            pltpu.SemaphoreType.DMA((13,)),
            pltpu.SemaphoreType.DMA((13,)),
            pltpu.SemaphoreType.DMA((4,)),
            pltpu.SemaphoreType.DMA((31,)),
            pltpu.SemaphoreType.DMA((31,)),
        ],
        compiler_params=pltpu.CompilerParams(collective_id=0, has_side_effects=True, vmem_limit_bytes=32 * 2**20),
        name="panel_sum",
    )(tiles, diag)


def gather_kernel(panel_ref, piece_ref, inv_ref, factor_ref, rows_ref, cols_ref, ending, send, recv, local_sem):
    s, r, c = (lax.axis_index(a) for a in ("scen", "row", "col"))
    y, k = r // 2, lax.rem(r, 2)
    rows = factor_ref.shape[0]
    to_col = 2 * s + y
    is_self = to_col == c
    barrier = pltpu.get_barrier_semaphore()
    for o in range(1, 4):
        pl.semaphore_signal(barrier, inc=1, device_id=(s, r, lax.rem(c + o, 4)), device_id_type=MESH_ID)
    for kk in range(2):
        for zz in range(4):
            src = (c // 2, 2 * lax.rem(c, 2) + kk, zz)

            @pl.when(jnp.logical_not(jnp.logical_and(is_self, jnp.logical_and(kk == k, zz == c))))
            def _():
                pl.semaphore_signal(barrier, inc=1, device_id=src, device_id_type=MESH_ID)

    f = panel_ref[0]
    first = (s * 4 + r) * (4 * rows) + c * rows
    for i in range(2):
        part = lax.dot_general(
            piece_ref[i], inv_ref[...], (((0,), (1,)), ((), ())),
            preferred_element_type=F32, precision=lax.Precision.HIGHEST,
        )
        ids = first + i * PANEL + lax.broadcasted_iota(jnp.int32, part.shape, 0)
        factor_ref[i * PANEL : (i + 1) * PANEL, :] = jnp.where(ids >= f * PANEL, part, 0.0)
        ending[i * PANEL : (i + 1) * PANEL, :] = jnp.where(ids >= f * PANEL + PANEL, part, 0.0).astype(BF16)

    pl.semaphore_wait(barrier, jnp.where(is_self, 10, 11))

    my_row = pl.ds(pl.multiple_of(c * rows, rows), rows)
    my_slot = k * 4 + c
    my_col = pl.ds(pl.multiple_of(my_slot * rows, rows), rows)
    sends = []
    n = 0
    for ds_ in range(2):
        for dr in range(4):
            dev = (lax.rem(s + 1 - ds_, 2), lax.rem(r + 3 - dr, 4), to_col)
            cp = remote(ending, cols_ref.at[my_col], send.at[n], recv.at[my_slot], dev)
            n += 1
            if ds_ == 1 and dr == 3:
                self_cp = cp
            else:
                cp.start()
                sends.append(cp)

    @pl.when(jnp.logical_not(is_self))
    def _():
        self_cp.start()

    for o in range(1, 4):
        cp = remote(ending, rows_ref.at[my_row], send.at[n], recv.at[7 + o], (s, r, lax.rem(c + o, 4)))
        cp.start()
        n += 1
        sends.append(cp)
    own_row = pltpu.make_async_copy(ending, rows_ref.at[my_row], local_sem.at[0])
    own_row.start()
    own_col = pltpu.make_async_copy(ending, cols_ref.at[my_col], local_sem.at[1])

    @pl.when(is_self)
    def _():
        own_col.start()

    for o in range(1, 4):
        at = pl.ds(pl.multiple_of(lax.rem(c + 4 - o, 4) * rows, rows), rows)
        remote(ending, rows_ref.at[at], send.at[0], recv.at[7 + o], (s, r, c)).wait_recv()
    for kk in range(2):
        for zz in range(4):
            i = kk * 4 + zz
            local_one = jnp.logical_and(is_self, jnp.logical_and(kk == k, zz == c))

            @pl.when(jnp.logical_not(local_one))
            def _():
                remote(ending, cols_ref.at[pl.ds(i * rows, rows)], send.at[0], recv.at[i], (s, r, c)).wait_recv()

    own_row.wait()

    @pl.when(is_self)
    def _():
        own_col.wait()

    for cp in sends:
        cp.wait_send()

    @pl.when(jnp.logical_not(is_self))
    def _():
        self_cp.wait_send()


def gathered(panel_index, piece, inverse, row_block, col_block):
    rows = 2 * PANEL
    vmem = pl.BlockSpec(memory_space=pltpu.VMEM)
    return pl.pallas_call(
        gather_kernel,
        out_shape=(
            jax.ShapeDtypeStruct((rows, PANEL), F32),
            jax.ShapeDtypeStruct((row_block, PANEL), BF16),
            jax.ShapeDtypeStruct((col_block, PANEL), BF16),
        ),
        in_specs=[pl.BlockSpec(memory_space=pltpu.SMEM), vmem, vmem],
        out_specs=(vmem, vmem, vmem),
        scratch_shapes=[
            pltpu.VMEM((rows, PANEL), BF16),
            pltpu.SemaphoreType.DMA((11,)),
            pltpu.SemaphoreType.DMA((11,)),
            pltpu.SemaphoreType.DMA((2,)),
        ],
        compiler_params=pltpu.CompilerParams(collective_id=1, has_side_effects=True),
        name="factor_gather",
    )(panel_index, piece, inverse)


def direct(root_matrix, inverse_block, link_tiles, tile_mask, panel_index):
    row_block, col_block = root_matrix.shape
    tiles, diag = scenario_tiles(root_matrix, inverse_block[0], link_tiles[0], tile_mask, panel_index)
    piece, diagonal = reduced(tiles, diag)
    chol_lower = jnp.linalg.cholesky(diagonal)
    inverse = jax.scipy.linalg.solve_triangular(chol_lower, jnp.eye(PANEL, dtype=F32), lower=True)
    factor_rows, own_rows, own_cols = gathered(panel_index, piece, inverse, row_block, col_block)
    update = lax.dot_general(
        own_rows, own_cols, (((1,), (1,)), ((), ())), preferred_element_type=jnp.float32
    )
    return (root_matrix - update, factor_rows)


def solution(mesh):
    in_specs = (
        P(("scen", "row"), "col"),
        P(("scen", "row", "col"), None, None),
        P(("scen", "row", "col"), None, None, None),
        P(("scen", "row", "col"), None),
        P(),
    )
    out_specs = (P(("scen", "row"), "col"), P(("scen", "row", "col"), None))
    sizes = tuple(mesh.shape[a] for a in ("scen", "row", "col"))
    body = direct if sizes == (2, 4, 4) else local
    return jax.shard_map(body, mesh=mesh, in_specs=in_specs, out_specs=out_specs, check_vma=False)
```

```python
import jax
import jax.numpy as jnp
from jax import lax
from jax.experimental import pallas as pl
from jax.experimental.pallas import tpu as pltpu
from jax.sharding import PartitionSpec as P

PANEL = 128


def broadcast(block, axis, source):
    block = jnp.where(lax.axis_index(axis) == source, block, jnp.zeros_like(block))
    return lax.psum(block, axis)


def select_matrix(tile_flags, slot_count):
    slot_order = jnp.cumsum(tile_flags) - 1
    slot_ids = lax.broadcasted_iota(jnp.int32, (slot_count, tile_flags.shape[0]), 0)
    hit = (slot_order[None, :] == slot_ids) & (tile_flags[None, :] == 1)
    return jnp.where(hit, jnp.float32(1.0), jnp.float32(0.0))


def compact_term(inverse, tiles_here, tile_flags, panel_at):
    slot_count, inner_rows, tile_rows = tiles_here.shape
    selector = select_matrix(tile_flags, slot_count)
    per_panel = PANEL // tile_rows
    picked = lax.dynamic_slice_in_dim(selector, panel_at * per_panel, per_panel, 1)
    columns = jnp.einsum(
        "kj,knt->njt", picked.astype(jnp.bfloat16), tiles_here, preferred_element_type=jnp.float32
    )
    columns = columns.reshape(inner_rows, PANEL).astype(jnp.bfloat16)
    weighted = jnp.dot(inverse, columns, preferred_element_type=jnp.float32).astype(jnp.bfloat16)
    product = jnp.einsum("knt,na->kta", tiles_here, weighted, preferred_element_type=jnp.float32)
    return (selector, product)


def dense_term(selector, product, base_cols, base_start):
    spread = jnp.einsum("kr,kta->rta", selector, product, precision=lax.Precision.HIGHEST)
    scenario = spread.reshape(selector.shape[1] * product.shape[1], PANEL)
    own_block = lax.dynamic_slice_in_dim(scenario, base_start, base_cols.shape[0], 0) + base_cols
    return lax.dynamic_update_slice_in_dim(scenario, own_block, base_start, 0)


def lower_rows(diagonal, rows_here, first_row, first_col):
    chol_lower = jnp.linalg.cholesky(diagonal)
    solved = jax.scipy.linalg.solve_triangular(chol_lower, rows_here.T, lower=True).T
    row_ids = first_row + lax.broadcasted_iota(jnp.int32, (rows_here.shape[0], 1), 0)
    return jnp.where(row_ids >= first_col, solved, 0.0)


def trailing_rows(factor_part, first_row, first_col):
    rounded = factor_part.astype(jnp.bfloat16)
    row_ids = first_row + lax.broadcasted_iota(jnp.int32, (factor_part.shape[0], 1), 0)
    return jnp.where(row_ids >= first_col + PANEL, rounded, jnp.zeros_like(rounded))


def local(root_matrix, inverse_block, link_tiles, tile_mask, panel_index):
    panel_at = panel_index[0]
    tile_flags = tile_mask[0]
    selector, product = compact_term(inverse_block[0], link_tiles[0], tile_flags, panel_at)
    tile_count = selector.shape[1]
    tile_rows = product.shape[1]
    total_rows = tile_count * tile_rows
    row_block, col_block = root_matrix.shape
    scen_at = lax.axis_index("scen")
    row_at = lax.axis_index("row")
    col_at = lax.axis_index("col")
    row_count = lax.axis_size("row")
    col_count = lax.axis_size("col")
    scen_count = lax.axis_size("scen")
    block_at = scen_at * row_count + row_at
    first_col = panel_at * PANEL
    owner_col = first_col // col_block
    base_cols = lax.dynamic_slice_in_dim(root_matrix, first_col - owner_col * col_block, PANEL, 1)
    base_cols = jnp.where(col_at == owner_col, base_cols, 0.0)
    piece_rows = row_block // col_count
    scenario = dense_term(selector, product, base_cols, block_at * row_block)
    slab_rows = total_rows // scen_count
    slab_sum = lax.psum_scatter(scenario, "scen", scatter_dimension=0, tiled=True)
    slab_sum = lax.psum(slab_sum, ("row", "col"))
    owner_slab = first_col // slab_rows
    diag_part = lax.dynamic_slice_in_dim(slab_sum, first_col - owner_slab * slab_rows, PANEL, 0)
    diagonal = broadcast(diag_part, "scen", owner_slab)
    slab_first = scen_at * slab_rows
    slab_factor = lower_rows(diagonal, slab_sum, slab_first, first_col)
    factor_rows = lax.dynamic_slice_in_dim(
        slab_factor, (row_at * col_count + col_at) * piece_rows, piece_rows, 0
    )
    ending = trailing_rows(slab_factor, slab_first, first_col)
    all_factor = lax.all_gather(ending, "scen", axis=0, tiled=True)
    own_rows = lax.dynamic_slice_in_dim(all_factor, block_at * row_block, row_block, 0)
    own_cols = lax.dynamic_slice_in_dim(all_factor, col_at * col_block, col_block, 0)
    update = lax.dot_general(
        own_rows, own_cols, (((1,), (1,)), ((), ())), preferred_element_type=jnp.float32
    )
    return (root_matrix - update, factor_rows)


MESH_ID = pl.DeviceIdType.MESH
F32 = jnp.float32
BF16 = jnp.bfloat16


def term_kernel(panel_ref, mask_ref, inv_hbm, tiles_hbm, root_ref, out_ref, diag_ref, inv, tiles, left, sems):
    slots = tiles.shape[0]
    f = panel_ref[0]
    scen_at, row_at, col_at = (lax.axis_index(a) for a in ("scen", "row", "col"))
    group = scen_at * lax.axis_size("row") + row_at
    inv_copy = pltpu.make_async_copy(inv_hbm, inv, sems.at[slots])
    inv_copy.start()

    def tile_copy(k):
        return pltpu.make_async_copy(tiles_hbm.at[k], tiles.at[k], sems.at[k])

    tile_total = mask_ref.shape[1]
    before = lax.fori_loop(0, f, lambda t, n: n + mask_ref[0, t], 0)
    total = lax.fori_loop(f, tile_total, lambda t, n: n + mask_ref[0, t], before)
    linked = mask_ref[0, f]
    first = jnp.minimum(before, slots - 1)
    panel_copy = pltpu.make_async_copy(tiles_hbm.at[first], left, sems.at[slots + 1])
    panel_copy.start()

    @pl.loop(0, total)
    def _(k):
        tile_copy(k).start()

    panel_copy.wait()
    columns = jnp.where(linked == 1, left[...], jnp.zeros_like(left))
    inv_copy.wait()
    weighted = lax.dot_general(
        columns, inv[...], (((0,), (0,)), ((), ())), preferred_element_type=F32
    ).astype(BF16)

    def one(t, at):
        flag = mask_ref[0, t]

        @pl.when(flag == 1)
        def _():
            tile_copy(at).wait()
            out_ref[t] = jnp.dot(weighted, tiles[at], preferred_element_type=F32)

        @pl.when(flag != 1)
        def _():
            out_ref[t] = jnp.zeros(out_ref.shape[1:], F32)

        return at + flag

    lax.fori_loop(0, tile_total, one, 0)
    own_tiles = root_ref.shape[0] // PANEL

    @pl.when(col_at == f // (tile_total // lax.axis_size("col")))
    def _():
        for i in range(own_tiles):
            at = group * own_tiles + i
            out_ref[at] = out_ref[at] + root_ref[i * PANEL : (i + 1) * PANEL, :].T

    diag_ref[...] = out_ref[f]


def scenario_tiles(root_matrix, inverse, tiles, tile_mask, panel_index):
    slots, inner, tile_rows = tiles.shape
    tile_total = tile_mask.shape[1]
    own_rows, own_cols = root_matrix.shape
    wide = own_cols // PANEL
    return pl.pallas_call(
        term_kernel,
        out_shape=(
            jax.ShapeDtypeStruct((tile_total, PANEL, tile_rows), F32),
            jax.ShapeDtypeStruct((PANEL, PANEL), F32),
        ),
        grid_spec=pltpu.PrefetchScalarGridSpec(
            num_scalar_prefetch=2,
            grid=(1,),
            in_specs=[
                pl.BlockSpec(memory_space=pltpu.HBM),
                pl.BlockSpec(memory_space=pltpu.HBM),
                pl.BlockSpec((own_rows, PANEL), lambda i, p, m: (0, lax.rem(p[0], wide))),
            ],
            out_specs=[
                pl.BlockSpec((tile_total, PANEL, tile_rows), lambda i, p, m: (0, 0, 0)),
                pl.BlockSpec((PANEL, PANEL), lambda i, p, m: (0, 0)),
            ],
            scratch_shapes=[
                pltpu.VMEM(inverse.shape, BF16),
                pltpu.VMEM(tiles.shape, BF16),
                pltpu.VMEM((inner, tile_rows), BF16),
                pltpu.SemaphoreType.DMA((slots + 2,)),
            ],
        ),
        compiler_params=pltpu.CompilerParams(vmem_limit_bytes=60 * 2**20),
        name="scenario_tiles",
    )(panel_index, tile_mask, inverse, tiles, root_matrix)


def remote(src, dst, send, recv, device):
    return pltpu.make_async_remote_copy(
        src_ref=src, dst_ref=dst, send_sem=send, recv_sem=recv, device_id=device, device_id_type=MESH_ID
    )


def sum_kernel(tiles_hbm, diag_in, piece_ref, diag_ref, own, got0, got1, got2, acc, got3, got4,
               dsum, dgot, dpart, dparts, send, recv, local_sem, dsend, drecv):
    s, r, c = (lax.axis_index(a) for a in ("scen", "row", "col"))
    y, k = r // 2, lax.rem(r, 2)
    core = (s, 2 * y + 1 - k, c)
    x_to = (1 - s, r, c)
    y_to = (s, 2 * (1 - y) + k, c)
    z1 = c + 1 - 2 * lax.rem(c, 2)
    z2 = lax.rem(c + 2, 4)
    me = s * 8 + y * 4 + c

    def chip(o):
        q = lax.rem(me + o, 16)
        return q, (q // 8, 2 * lax.rem(q // 4, 2) + k, lax.rem(q, 4))

    barrier = pltpu.get_barrier_semaphore()
    pl.semaphore_signal(barrier, inc=1, device_id=core, device_id_type=MESH_ID)
    for o in range(1, 16):
        pl.semaphore_signal(barrier, inc=1, device_id=chip(o)[1], device_id_type=MESH_ID)
    pl.semaphore_wait(barrier, 16)

    core_diag = remote(diag_in, dgot, dsend.at[0], drecv.at[0], core)
    core_diag.start()
    core_copy = []
    loads = []
    for sp in range(2):
        for yp in range(2):
            i = sp * 2 + yp
            cp = remote(tiles_hbm.at[pl.ds((i * 2 + 1 - k) * 8, 8)], got0.at[i], send.at[i], recv.at[i], core)
            cp.start()
            core_copy.append(cp)
            ld = pltpu.make_async_copy(tiles_hbm.at[pl.ds((i * 2 + k) * 8, 8)], own.at[i], local_sem.at[i])
            ld.start()
            loads.append(ld)
    core_diag.wait()
    dsum[...] = diag_in[...] + dgot[...]
    out1 = []
    for o in range(1, 16):
        q, dev = chip(o)
        cp = remote(dsum.at[pl.ds(pl.multiple_of(q * 8, 8), 8)], dparts.at[o], dsend.at[o], drecv.at[o], dev)
        cp.start()
        out1.append(cp)
    for i in range(4):
        loads[i].wait()
        core_copy[i].wait()
        own[i] = own[i] + got0[i]
    order = []
    ax = []
    for step in range(2):
        yy = (1 - y) if step == 0 else y
        ss = (1 - s) if step == 0 else s
        a = remote(own.at[(1 - s) * 2 + yy, pl.ds(0, 4)], got1.at[0, step], send.at[4 + step], recv.at[4 + step], x_to)
        b = remote(own.at[ss * 2 + 1 - y, pl.ds(4, 4)], got1.at[1, step], send.at[6 + step], recv.at[6 + step], y_to)
        a.start()
        b.start()
        ax.append((a, b))
    for cp in out1:
        cp.wait_recv()
    total = dsum[pl.ds(pl.multiple_of(me * 8, 8), 8), :]
    for o in range(1, 16):
        total = total + dparts[o]
    dpart[...] = total
    diag_ref[pl.ds(pl.multiple_of(me * 8, 8), 8), :] = total
    out2 = []
    for o in range(1, 16):
        q, dev = chip(o)
        cp = remote(dpart, diag_ref.at[pl.ds(pl.multiple_of(me * 8, 8), 8)], dsend.at[15 + o], drecv.at[15 + o], dev)
        cp.start()
        out2.append(cp)
    ax[0][0].wait_recv()
    acc[0, 0] = own[s * 2 + 1 - y, 0:4] + got1[0, 0]
    a2 = remote(acc.at[0, 0], got2.at[0], send.at[8], recv.at[8], y_to)
    a2.start()
    ax[0][1].wait_recv()
    acc[0, 1] = own[(1 - s) * 2 + y, 4:8] + got1[1, 0]
    b2 = remote(acc.at[0, 1], got2.at[1], send.at[9], recv.at[9], x_to)
    b2.start()
    ax[1][0].wait_recv()
    acc[1, 0] = own[s * 2 + y, 0:4] + got1[0, 1]
    ax[1][1].wait_recv()
    acc[1, 1] = own[s * 2 + y, 4:8] + got1[1, 1]
    a2.wait_recv()
    acc[1, 0] = acc[1, 0] + got2[0]
    b2.wait_recv()
    acc[1, 1] = acc[1, 1] + got2[1]
    par = lax.rem(c, 2)
    hi = c // 2
    z_out = []
    for h in range(2):
        cp = remote(acc.at[1, h, pl.ds((1 - par) * 2, 2)], got3.at[h], send.at[10 + h], recv.at[10 + h], (s, r, z1))
        cp.start()
        z_out.append(cp)
    z_out[0].wait_recv()
    z_out[1].wait_recv()
    a2.wait_send()
    acc[0, 0, pl.ds(0, 2)] = acc[1, 1 - hi, pl.ds(par * 2, 2)] + got3[1 - hi]
    last = remote(acc.at[0, 0, pl.ds(0, 2)], got4, send.at[12], recv.at[12], (s, r, z2))
    last.start()
    mine = acc[1, hi, pl.ds(par * 2, 2)] + got3[hi]
    last.wait_recv()
    piece_ref[...] = mine + got4[...]
    for cp in out2:
        cp.wait_recv()
    for cp in out1 + out2 + [ax[0][0], ax[0][1], ax[1][0], ax[1][1], b2, *z_out, last]:
        cp.wait_send()


def reduced(tiles, diag):
    tile = tiles.shape[1:]
    vmem = pl.BlockSpec(memory_space=pltpu.VMEM)
    return pl.pallas_call(
        sum_kernel,
        out_shape=(jax.ShapeDtypeStruct((2, *tile), F32), jax.ShapeDtypeStruct((PANEL, PANEL), F32)),
        in_specs=[pl.BlockSpec(memory_space=pl.ANY), vmem],
        out_specs=(vmem, vmem),
        scratch_shapes=[
            pltpu.VMEM((4, 8, *tile), F32),
            pltpu.VMEM((4, 8, *tile), F32),
            pltpu.VMEM((2, 2, 4, *tile), F32),
            pltpu.VMEM((2, 4, *tile), F32),
            pltpu.VMEM((2, 2, 4, *tile), F32),
            pltpu.VMEM((2, 2, *tile), F32),
            pltpu.VMEM((2, *tile), F32),
            pltpu.VMEM(tile, F32),
            pltpu.VMEM(tile, F32),
            pltpu.VMEM((8, PANEL), F32),
            pltpu.VMEM((16, 8, PANEL), F32),
            pltpu.SemaphoreType.DMA((13,)),
            pltpu.SemaphoreType.DMA((13,)),
            pltpu.SemaphoreType.DMA((4,)),
            pltpu.SemaphoreType.DMA((31,)),
            pltpu.SemaphoreType.DMA((31,)),
        ],
        compiler_params=pltpu.CompilerParams(collective_id=0, has_side_effects=True, vmem_limit_bytes=32 * 2**20),
        name="panel_sum",
    )(tiles, diag)


def gather_kernel(panel_ref, piece_ref, inv_ref, factor_ref, rows_ref, cols_ref, send_z, recv_z,
                  send_x, send_y, recv_p, send_c, recv_c):
    s, r, c = (lax.axis_index(a) for a in ("scen", "row", "col"))
    y, k = r // 2, lax.rem(r, 2)
    rows = factor_ref.shape[0]
    far_x = lax.rem(s + c // 2, 2)
    far_y = lax.rem(y + c, 2)
    source = jnp.logical_and(far_x == 0, far_y == 0)
    x_to = (1 - s, r, c)
    y_to = (s, 2 * (1 - y) + k, c)
    core = (s, 2 * y + 1 - k, c)
    barrier = pltpu.get_barrier_semaphore()
    for o in range(1, 4):
        pl.semaphore_signal(barrier, inc=1, device_id=(s, r, lax.rem(c + o, 4)), device_id_type=MESH_ID)
    for dev in (x_to, y_to, core):
        pl.semaphore_signal(barrier, inc=1, device_id=dev, device_id_type=MESH_ID)

    def row_at(z):
        return rows_ref.at[pl.ds(pl.multiple_of(z * rows, rows), rows)]

    def col_at(kk, z):
        return cols_ref.at[pl.ds(pl.multiple_of((kk * 4 + z) * rows, rows), rows)]

    f = panel_ref[0]
    first = (s * 4 + r) * (4 * rows) + c * rows
    for i in range(2):
        part = lax.dot_general(
            piece_ref[i], inv_ref[...], (((0,), (1,)), ((), ())),
            preferred_element_type=F32, precision=lax.Precision.HIGHEST,
        )
        ids = first + i * PANEL + lax.broadcasted_iota(jnp.int32, part.shape, 0)
        factor_ref[i * PANEL : (i + 1) * PANEL, :] = jnp.where(ids >= f * PANEL, part, 0.0)
        ending = jnp.where(ids >= f * PANEL + PANEL, part, 0.0).astype(BF16)
        rows_ref[pl.ds(pl.multiple_of(c * rows + i * PANEL, PANEL), PANEL), :] = ending

    pl.semaphore_wait(barrier, 6)
    z_copies = []
    for o in range(1, 4):
        cp = remote(row_at(c), row_at(c), send_z.at[o - 1], recv_z.at[o - 1], (s, r, lax.rem(c + o, 4)))
        cp.start()
        z_copies.append(cp)

    def z_arrival(o):
        remote(row_at(lax.rem(c + 4 - o, 4)), row_at(lax.rem(c + 4 - o, 4)), send_z.at[o - 1], recv_z.at[o - 1], core).wait_recv()

    for o in range(4):
        z = lax.rem(c + 4 - o, 4)
        here = col_at(k, z)
        to_x = remote(here, here, send_x.at[o], recv_p.at[o], x_to)
        to_y = remote(here, here, send_y.at[o], recv_p.at[o], y_to)

        @pl.when(source)
        def _():
            if o:
                z_arrival(o)
            here[...] = row_at(z)[...]
            to_x.start()
            to_y.start()

        @pl.when(jnp.logical_not(source))
        def _():
            to_x.wait_recv()

        @pl.when(jnp.logical_and(far_x == 1, far_y == 0) if o < 2 else jnp.logical_and(far_x == 0, far_y == 1))
        def _():
            (to_y if o < 2 else to_x).start()

        remote(here, here, send_c.at[o], recv_c.at[o], core).start()

    @pl.when(jnp.logical_not(source))
    def _():
        for o in range(1, 4):
            z_arrival(o)

    for o in range(4):
        z = lax.rem(c + 4 - o, 4)
        there, here = col_at(1 - k, z), col_at(k, z)
        remote(there, there, send_c.at[o], recv_c.at[o], core).wait_recv()
        remote(here, here, send_c.at[o], recv_c.at[o], core).wait_send()
        to_x = remote(here, here, send_x.at[o], recv_p.at[o], x_to)
        to_y = remote(here, here, send_y.at[o], recv_p.at[o], y_to)

        @pl.when(source)
        def _():
            to_x.wait_send()
            to_y.wait_send()

        @pl.when(jnp.logical_and(far_x == 1, far_y == 0) if o < 2 else jnp.logical_and(far_x == 0, far_y == 1))
        def _():
            (to_y if o < 2 else to_x).wait_send()

    for cp in z_copies:
        cp.wait_send()


def gathered(panel_index, piece, inverse, row_block, col_block):
    rows = 2 * PANEL
    vmem = pl.BlockSpec(memory_space=pltpu.VMEM)
    return pl.pallas_call(
        gather_kernel,
        out_shape=(
            jax.ShapeDtypeStruct((rows, PANEL), F32),
            jax.ShapeDtypeStruct((row_block, PANEL), BF16),
            jax.ShapeDtypeStruct((col_block, PANEL), BF16),
        ),
        in_specs=[pl.BlockSpec(memory_space=pltpu.SMEM), vmem, vmem],
        out_specs=(vmem, vmem, vmem),
        scratch_shapes=[
            pltpu.SemaphoreType.DMA((3,)),
            pltpu.SemaphoreType.DMA((3,)),
            pltpu.SemaphoreType.DMA((4,)),
            pltpu.SemaphoreType.DMA((4,)),
            pltpu.SemaphoreType.DMA((4,)),
            pltpu.SemaphoreType.DMA((4,)),
            pltpu.SemaphoreType.DMA((4,)),
        ],
        compiler_params=pltpu.CompilerParams(collective_id=1, has_side_effects=True),
        name="factor_gather",
    )(panel_index, piece, inverse)


def direct(root_matrix, inverse_block, link_tiles, tile_mask, panel_index):
    row_block, col_block = root_matrix.shape
    tiles, diag = scenario_tiles(root_matrix, inverse_block[0], link_tiles[0], tile_mask, panel_index)
    piece, diagonal = reduced(tiles, diag)
    chol_lower = jnp.linalg.cholesky(diagonal)
    inverse = jax.scipy.linalg.solve_triangular(chol_lower, jnp.eye(PANEL, dtype=F32), lower=True)
    factor_rows, own_rows, own_cols = gathered(panel_index, piece, inverse, row_block, col_block)
    update = lax.dot_general(
        own_rows, own_cols, (((1,), (1,)), ((), ())), preferred_element_type=jnp.float32
    )
    return (root_matrix - update, factor_rows)


def solution(mesh):
    in_specs = (
        P(("scen", "row"), "col"),
        P(("scen", "row", "col"), None, None),
        P(("scen", "row", "col"), None, None, None),
        P(("scen", "row", "col"), None),
        P(),
    )
    out_specs = (P(("scen", "row"), "col"), P(("scen", "row", "col"), None))
    sizes = tuple(mesh.shape[a] for a in ("scen", "row", "col"))
    body = direct if sizes == (2, 4, 4) else local
    return jax.shard_map(body, mesh=mesh, in_specs=in_specs, out_specs=out_specs, check_vma=False)
```

```python
import jax
import jax.numpy as jnp
from jax import lax
from jax.experimental import pallas as pl
from jax.experimental.pallas import tpu as pltpu
from jax.sharding import PartitionSpec as P

PANEL = 128


def broadcast(block, axis, source):
    block = jnp.where(lax.axis_index(axis) == source, block, jnp.zeros_like(block))
    return lax.psum(block, axis)


def select_matrix(tile_flags, slot_count):
    slot_order = jnp.cumsum(tile_flags) - 1
    slot_ids = lax.broadcasted_iota(jnp.int32, (slot_count, tile_flags.shape[0]), 0)
    hit = (slot_order[None, :] == slot_ids) & (tile_flags[None, :] == 1)
    return jnp.where(hit, jnp.float32(1.0), jnp.float32(0.0))


def compact_term(inverse, tiles_here, tile_flags, panel_at):
    slot_count, inner_rows, tile_rows = tiles_here.shape
    selector = select_matrix(tile_flags, slot_count)
    per_panel = PANEL // tile_rows
    picked = lax.dynamic_slice_in_dim(selector, panel_at * per_panel, per_panel, 1)
    columns = jnp.einsum(
        "kj,knt->njt", picked.astype(jnp.bfloat16), tiles_here, preferred_element_type=jnp.float32
    )
    columns = columns.reshape(inner_rows, PANEL).astype(jnp.bfloat16)
    weighted = jnp.dot(inverse, columns, preferred_element_type=jnp.float32).astype(jnp.bfloat16)
    product = jnp.einsum("knt,na->kta", tiles_here, weighted, preferred_element_type=jnp.float32)
    return (selector, product)


def dense_term(selector, product, base_cols, base_start):
    spread = jnp.einsum("kr,kta->rta", selector, product, precision=lax.Precision.HIGHEST)
    scenario = spread.reshape(selector.shape[1] * product.shape[1], PANEL)
    own_block = lax.dynamic_slice_in_dim(scenario, base_start, base_cols.shape[0], 0) + base_cols
    return lax.dynamic_update_slice_in_dim(scenario, own_block, base_start, 0)


def lower_rows(diagonal, rows_here, first_row, first_col):
    chol_lower = jnp.linalg.cholesky(diagonal)
    solved = jax.scipy.linalg.solve_triangular(chol_lower, rows_here.T, lower=True).T
    row_ids = first_row + lax.broadcasted_iota(jnp.int32, (rows_here.shape[0], 1), 0)
    return jnp.where(row_ids >= first_col, solved, 0.0)


def trailing_rows(factor_part, first_row, first_col):
    rounded = factor_part.astype(jnp.bfloat16)
    row_ids = first_row + lax.broadcasted_iota(jnp.int32, (factor_part.shape[0], 1), 0)
    return jnp.where(row_ids >= first_col + PANEL, rounded, jnp.zeros_like(rounded))


def local(root_matrix, inverse_block, link_tiles, tile_mask, panel_index):
    panel_at = panel_index[0]
    tile_flags = tile_mask[0]
    selector, product = compact_term(inverse_block[0], link_tiles[0], tile_flags, panel_at)
    tile_count = selector.shape[1]
    tile_rows = product.shape[1]
    total_rows = tile_count * tile_rows
    row_block, col_block = root_matrix.shape
    scen_at = lax.axis_index("scen")
    row_at = lax.axis_index("row")
    col_at = lax.axis_index("col")
    row_count = lax.axis_size("row")
    col_count = lax.axis_size("col")
    scen_count = lax.axis_size("scen")
    block_at = scen_at * row_count + row_at
    first_col = panel_at * PANEL
    owner_col = first_col // col_block
    base_cols = lax.dynamic_slice_in_dim(root_matrix, first_col - owner_col * col_block, PANEL, 1)
    base_cols = jnp.where(col_at == owner_col, base_cols, 0.0)
    piece_rows = row_block // col_count
    scenario = dense_term(selector, product, base_cols, block_at * row_block)
    slab_rows = total_rows // scen_count
    slab_sum = lax.psum_scatter(scenario, "scen", scatter_dimension=0, tiled=True)
    slab_sum = lax.psum(slab_sum, ("row", "col"))
    owner_slab = first_col // slab_rows
    diag_part = lax.dynamic_slice_in_dim(slab_sum, first_col - owner_slab * slab_rows, PANEL, 0)
    diagonal = broadcast(diag_part, "scen", owner_slab)
    slab_first = scen_at * slab_rows
    slab_factor = lower_rows(diagonal, slab_sum, slab_first, first_col)
    factor_rows = lax.dynamic_slice_in_dim(
        slab_factor, (row_at * col_count + col_at) * piece_rows, piece_rows, 0
    )
    ending = trailing_rows(slab_factor, slab_first, first_col)
    all_factor = lax.all_gather(ending, "scen", axis=0, tiled=True)
    own_rows = lax.dynamic_slice_in_dim(all_factor, block_at * row_block, row_block, 0)
    own_cols = lax.dynamic_slice_in_dim(all_factor, col_at * col_block, col_block, 0)
    update = lax.dot_general(
        own_rows, own_cols, (((1,), (1,)), ((), ())), preferred_element_type=jnp.float32
    )
    return (root_matrix - update, factor_rows)


MESH_ID = pl.DeviceIdType.MESH
F32 = jnp.float32
BF16 = jnp.bfloat16


def term_kernel(panel_ref, mask_ref, inv_hbm, tiles_hbm, root_ref, out_ref, diag_ref, inv, tiles, left, sems):
    slots = tiles.shape[0]
    f = panel_ref[0]
    scen_at, row_at, col_at = (lax.axis_index(a) for a in ("scen", "row", "col"))
    group = scen_at * lax.axis_size("row") + row_at
    inv_copy = pltpu.make_async_copy(inv_hbm, inv, sems.at[slots])
    inv_copy.start()

    def tile_copy(k):
        return pltpu.make_async_copy(tiles_hbm.at[k], tiles.at[k], sems.at[k])

    tile_total = mask_ref.shape[1]
    before = lax.fori_loop(0, f, lambda t, n: n + mask_ref[0, t], 0)
    total = lax.fori_loop(f, tile_total, lambda t, n: n + mask_ref[0, t], before)
    linked = mask_ref[0, f]
    first = jnp.minimum(before, slots - 1)
    panel_copy = pltpu.make_async_copy(tiles_hbm.at[first], left, sems.at[slots + 1])
    panel_copy.start()

    @pl.loop(0, total)
    def _(k):
        tile_copy(k).start()

    panel_copy.wait()
    columns = jnp.where(linked == 1, left[...], jnp.zeros_like(left))
    inv_copy.wait()
    weighted = lax.dot_general(
        columns, inv[...], (((0,), (0,)), ((), ())), preferred_element_type=F32
    ).astype(BF16)

    def one(t, at):
        flag = mask_ref[0, t]

        @pl.when(flag == 1)
        def _():
            tile_copy(at).wait()
            out_ref[t] = jnp.dot(weighted, tiles[at], preferred_element_type=F32)

        @pl.when(flag != 1)
        def _():
            out_ref[t] = jnp.zeros(out_ref.shape[1:], F32)

        return at + flag

    lax.fori_loop(0, tile_total, one, 0)
    own_tiles = root_ref.shape[0] // PANEL

    @pl.when(col_at == f // (tile_total // lax.axis_size("col")))
    def _():
        for i in range(own_tiles):
            at = group * own_tiles + i
            out_ref[at] = out_ref[at] + root_ref[i * PANEL : (i + 1) * PANEL, :].T

    diag_ref[...] = out_ref[f]


def scenario_tiles(root_matrix, inverse, tiles, tile_mask, panel_index):
    slots, inner, tile_rows = tiles.shape
    tile_total = tile_mask.shape[1]
    own_rows, own_cols = root_matrix.shape
    wide = own_cols // PANEL
    return pl.pallas_call(
        term_kernel,
        out_shape=(
            jax.ShapeDtypeStruct((tile_total, PANEL, tile_rows), F32),
            jax.ShapeDtypeStruct((PANEL, PANEL), F32),
        ),
        grid_spec=pltpu.PrefetchScalarGridSpec(
            num_scalar_prefetch=2,
            grid=(1,),
            in_specs=[
                pl.BlockSpec(memory_space=pltpu.HBM),
                pl.BlockSpec(memory_space=pltpu.HBM),
                pl.BlockSpec((own_rows, PANEL), lambda i, p, m: (0, lax.rem(p[0], wide))),
            ],
            out_specs=[
                pl.BlockSpec((tile_total, PANEL, tile_rows), lambda i, p, m: (0, 0, 0)),
                pl.BlockSpec((PANEL, PANEL), lambda i, p, m: (0, 0)),
            ],
            scratch_shapes=[
                pltpu.VMEM(inverse.shape, BF16),
                pltpu.VMEM(tiles.shape, BF16),
                pltpu.VMEM((inner, tile_rows), BF16),
                pltpu.SemaphoreType.DMA((slots + 2,)),
            ],
        ),
        compiler_params=pltpu.CompilerParams(vmem_limit_bytes=60 * 2**20),
        name="scenario_tiles",
    )(panel_index, tile_mask, inverse, tiles, root_matrix)


def remote(src, dst, send, recv, device):
    return pltpu.make_async_remote_copy(
        src_ref=src, dst_ref=dst, send_sem=send, recv_sem=recv, device_id=device, device_id_type=MESH_ID
    )


def invert_blocks(state, inv_ref, start, stop):
    lane = lax.broadcasted_iota(jnp.int32, (8, PANEL), 1)
    sub = lax.broadcasted_iota(jnp.int32, (8, 1), 0)

    def block(b, carry):
        at = pl.ds(pl.multiple_of(b * 8, 8), 8)
        strip = state[at, :]
        for i in range(8):
            col = jnp.sum(jnp.where(lane == b * 8 + i, strip[:, :PANEL], 0.0), axis=1, keepdims=True)
            pivot = col[i : i + 1, :]
            inv = lax.rsqrt(pivot)
            inv = inv * (1.5 - 0.5 * pivot * inv * inv)
            row = strip[i : i + 1, :] * inv
            coef = jnp.where(sub > i, col * inv, 0.0)
            strip = jnp.where(sub == i, row, strip - coef * row)
        inv_ref[at, :] = strip[:, PANEL:]
        later = jnp.where(lane >= b * 8 + 8, strip[:, :PANEL], 0.0)
        state[...] = state[...] - lax.dot_general(
            later, strip, (((0,), (0,)), ((), ())), preferred_element_type=F32, precision=lax.Precision.HIGHEST
        )
        return carry

    lax.fori_loop(start, stop, block, 0)


def gather_phase(panel_ref, piece_ref, inv_ref, factor_ref, rows_ref, cols_ref, send_z, recv_z,
                 send_x, send_y, recv_p, send_c, recv_c):
    s, r, c = (lax.axis_index(a) for a in ("scen", "row", "col"))
    y, k = r // 2, lax.rem(r, 2)
    rows = factor_ref.shape[0]
    far_x = lax.rem(s + c // 2, 2)
    far_y = lax.rem(y + c, 2)
    source = jnp.logical_and(far_x == 0, far_y == 0)
    x_to = (1 - s, r, c)
    y_to = (s, 2 * (1 - y) + k, c)
    core = (s, 2 * y + 1 - k, c)

    def row_at(z):
        return rows_ref.at[pl.ds(pl.multiple_of(z * rows, rows), rows)]

    def col_at(kk, z):
        return cols_ref.at[pl.ds(pl.multiple_of((kk * 4 + z) * rows, rows), rows)]

    f = panel_ref[0]
    first = (s * 4 + r) * (4 * rows) + c * rows
    for i in range(2):
        part = lax.dot_general(
            piece_ref[i], inv_ref[...], (((0,), (1,)), ((), ())),
            preferred_element_type=F32, precision=lax.Precision.HIGHEST,
        )
        ids = first + i * PANEL + lax.broadcasted_iota(jnp.int32, part.shape, 0)
        factor_ref[i * PANEL : (i + 1) * PANEL, :] = jnp.where(ids >= f * PANEL, part, 0.0)
        ending = jnp.where(ids >= f * PANEL + PANEL, part, 0.0).astype(BF16)
        rows_ref[pl.ds(pl.multiple_of(c * rows + i * PANEL, PANEL), PANEL), :] = ending

    z_copies = []
    for o in range(1, 4):
        cp = remote(row_at(c), row_at(c), send_z.at[o - 1], recv_z.at[o - 1], (s, r, lax.rem(c + o, 4)))
        cp.start()
        z_copies.append(cp)

    def z_arrival(o):
        remote(row_at(lax.rem(c + 4 - o, 4)), row_at(lax.rem(c + 4 - o, 4)), send_z.at[o - 1], recv_z.at[o - 1], core).wait_recv()

    for o in range(4):
        z = lax.rem(c + 4 - o, 4)
        here = col_at(k, z)
        to_x = remote(here, here, send_x.at[o], recv_p.at[o], x_to)
        to_y = remote(here, here, send_y.at[o], recv_p.at[o], y_to)

        @pl.when(source)
        def _():
            if o:
                z_arrival(o)
            here[...] = row_at(z)[...]
            to_x.start()
            to_y.start()

        @pl.when(jnp.logical_not(source))
        def _():
            to_x.wait_recv()

        @pl.when(jnp.logical_and(far_x == 1, far_y == 0) if o < 2 else jnp.logical_and(far_x == 0, far_y == 1))
        def _():
            (to_y if o < 2 else to_x).start()

        remote(here, here, send_c.at[o], recv_c.at[o], core).start()

    @pl.when(jnp.logical_not(source))
    def _():
        for o in range(1, 4):
            z_arrival(o)

    for o in range(4):
        z = lax.rem(c + 4 - o, 4)
        there, here = col_at(1 - k, z), col_at(k, z)
        remote(there, there, send_c.at[o], recv_c.at[o], core).wait_recv()
        remote(here, here, send_c.at[o], recv_c.at[o], core).wait_send()
        to_x = remote(here, here, send_x.at[o], recv_p.at[o], x_to)
        to_y = remote(here, here, send_y.at[o], recv_p.at[o], y_to)

        @pl.when(source)
        def _():
            to_x.wait_send()
            to_y.wait_send()

        @pl.when(jnp.logical_and(far_x == 1, far_y == 0) if o < 2 else jnp.logical_and(far_x == 0, far_y == 1))
        def _():
            (to_y if o < 2 else to_x).wait_send()

    for cp in z_copies:
        cp.wait_send()


def panel_kernel(panel_ref, tiles_hbm, diag_in, factor_ref, rows_ref, cols_ref, own, got0, got1, got2, acc, got3, got4,
                 dsum, dgot, dpart, dparts, diag_ref, state, inv_ref, piece_ref, send, recv, local_sem, dsend, drecv,
                 *gather_sems):
    s, r, c = (lax.axis_index(a) for a in ("scen", "row", "col"))
    y, k = r // 2, lax.rem(r, 2)
    core = (s, 2 * y + 1 - k, c)
    x_to = (1 - s, r, c)
    y_to = (s, 2 * (1 - y) + k, c)
    z1 = c + 1 - 2 * lax.rem(c, 2)
    z2 = lax.rem(c + 2, 4)
    me = s * 8 + y * 4 + c

    def chip(o):
        q = lax.rem(me + o, 16)
        return q, (q // 8, 2 * lax.rem(q // 4, 2) + k, lax.rem(q, 4))

    barrier = pltpu.get_barrier_semaphore()
    pl.semaphore_signal(barrier, inc=1, device_id=core, device_id_type=MESH_ID)
    for o in range(1, 16):
        pl.semaphore_signal(barrier, inc=1, device_id=chip(o)[1], device_id_type=MESH_ID)
    pl.semaphore_wait(barrier, 16)

    core_diag = remote(diag_in, dgot, dsend.at[0], drecv.at[0], core)
    core_diag.start()
    core_copy = []
    loads = []
    for sp in range(2):
        for yp in range(2):
            i = sp * 2 + yp
            cp = remote(tiles_hbm.at[pl.ds((i * 2 + 1 - k) * 8, 8)], got0.at[i], send.at[i], recv.at[i], core)
            cp.start()
            core_copy.append(cp)
            ld = pltpu.make_async_copy(tiles_hbm.at[pl.ds((i * 2 + k) * 8, 8)], own.at[i], local_sem.at[i])
            ld.start()
            loads.append(ld)
    core_diag.wait()
    dsum[...] = diag_in[...] + dgot[...]
    out1 = []
    for o in range(1, 16):
        q, dev = chip(o)
        cp = remote(dsum.at[pl.ds(pl.multiple_of(q * 8, 8), 8)], dparts.at[o], dsend.at[o], drecv.at[o], dev)
        cp.start()
        out1.append(cp)
    for i in range(4):
        loads[i].wait()
        core_copy[i].wait()
        own[i] = own[i] + got0[i]
    order = []
    ax = []
    for step in range(2):
        yy = (1 - y) if step == 0 else y
        ss = (1 - s) if step == 0 else s
        a = remote(own.at[(1 - s) * 2 + yy, pl.ds(0, 4)], got1.at[0, step], send.at[4 + step], recv.at[4 + step], x_to)
        b = remote(own.at[ss * 2 + 1 - y, pl.ds(4, 4)], got1.at[1, step], send.at[6 + step], recv.at[6 + step], y_to)
        a.start()
        b.start()
        ax.append((a, b))
    for cp in out1:
        cp.wait_recv()
    total = dsum[pl.ds(pl.multiple_of(me * 8, 8), 8), :]
    for o in range(1, 16):
        total = total + dparts[o]
    dpart[...] = total
    diag_ref[pl.ds(pl.multiple_of(me * 8, 8), 8), :] = total
    out2 = []
    for o in range(1, 16):
        q, dev = chip(o)
        cp = remote(dpart, diag_ref.at[pl.ds(pl.multiple_of(me * 8, 8), 8)], dsend.at[15 + o], drecv.at[15 + o], dev)
        cp.start()
        out2.append(cp)
    for cp in out2:
        cp.wait_recv()
    full = diag_ref[...]
    state[:, :PANEL] = 0.5 * (full + full.T)
    state[:, PANEL:] = jnp.where(
        lax.broadcasted_iota(jnp.int32, (PANEL, PANEL), 0) == lax.broadcasted_iota(jnp.int32, (PANEL, PANEL), 1), 1.0, 0.0
    )
    invert_blocks(state, inv_ref, 0, 3)
    ax[0][0].wait_recv()
    acc[0, 0] = own[s * 2 + 1 - y, 0:4] + got1[0, 0]
    a2 = remote(acc.at[0, 0], got2.at[0], send.at[8], recv.at[8], y_to)
    a2.start()
    ax[0][1].wait_recv()
    acc[0, 1] = own[(1 - s) * 2 + y, 4:8] + got1[1, 0]
    b2 = remote(acc.at[0, 1], got2.at[1], send.at[9], recv.at[9], x_to)
    b2.start()
    invert_blocks(state, inv_ref, 3, 9)
    ax[1][0].wait_recv()
    acc[1, 0] = own[s * 2 + y, 0:4] + got1[0, 1]
    ax[1][1].wait_recv()
    acc[1, 1] = own[s * 2 + y, 4:8] + got1[1, 1]
    a2.wait_recv()
    acc[1, 0] = acc[1, 0] + got2[0]
    b2.wait_recv()
    acc[1, 1] = acc[1, 1] + got2[1]
    par = lax.rem(c, 2)
    hi = c // 2
    z_out = []
    for h in range(2):
        cp = remote(acc.at[1, h, pl.ds((1 - par) * 2, 2)], got3.at[h], send.at[10 + h], recv.at[10 + h], (s, r, z1))
        cp.start()
        z_out.append(cp)
    invert_blocks(state, inv_ref, 9, 13)
    z_out[0].wait_recv()
    z_out[1].wait_recv()
    a2.wait_send()
    acc[0, 0, pl.ds(0, 2)] = acc[1, 1 - hi, pl.ds(par * 2, 2)] + got3[1 - hi]
    last = remote(acc.at[0, 0, pl.ds(0, 2)], got4, send.at[12], recv.at[12], (s, r, z2))
    last.start()
    mine = acc[1, hi, pl.ds(par * 2, 2)] + got3[hi]
    invert_blocks(state, inv_ref, 13, 16)
    last.wait_recv()
    piece_ref[...] = mine + got4[...]
    gather_phase(panel_ref, piece_ref, inv_ref, factor_ref, rows_ref, cols_ref, *gather_sems)
    for cp in out1 + out2 + [ax[0][0], ax[0][1], ax[1][0], ax[1][1], b2, *z_out, last]:
        cp.wait_send()


def panel_factor(panel_index, tiles, diag, row_block, col_block):
    tile = tiles.shape[1:]
    vmem = pl.BlockSpec(memory_space=pltpu.VMEM)
    return pl.pallas_call(
        panel_kernel,
        out_shape=(
            jax.ShapeDtypeStruct((2 * PANEL, PANEL), F32),
            jax.ShapeDtypeStruct((row_block, PANEL), BF16),
            jax.ShapeDtypeStruct((col_block, PANEL), BF16),
        ),
        in_specs=[pl.BlockSpec(memory_space=pltpu.SMEM), pl.BlockSpec(memory_space=pl.ANY), vmem],
        out_specs=(vmem, vmem, vmem),
        scratch_shapes=[
            pltpu.VMEM((4, 8, *tile), F32),
            pltpu.VMEM((4, 8, *tile), F32),
            pltpu.VMEM((2, 2, 4, *tile), F32),
            pltpu.VMEM((2, 4, *tile), F32),
            pltpu.VMEM((2, 2, 4, *tile), F32),
            pltpu.VMEM((2, 2, *tile), F32),
            pltpu.VMEM((2, *tile), F32),
            pltpu.VMEM(tile, F32),
            pltpu.VMEM(tile, F32),
            pltpu.VMEM((8, PANEL), F32),
            pltpu.VMEM((16, 8, PANEL), F32),
            pltpu.VMEM(tile, F32),
            pltpu.VMEM((PANEL, 2 * PANEL), F32),
            pltpu.VMEM(tile, F32),
            pltpu.VMEM((2, *tile), F32),
            pltpu.SemaphoreType.DMA((13,)),
            pltpu.SemaphoreType.DMA((13,)),
            pltpu.SemaphoreType.DMA((4,)),
            pltpu.SemaphoreType.DMA((31,)),
            pltpu.SemaphoreType.DMA((31,)),
            pltpu.SemaphoreType.DMA((3,)),
            pltpu.SemaphoreType.DMA((3,)),
            *[pltpu.SemaphoreType.DMA((4,))] * 5,
        ],
        compiler_params=pltpu.CompilerParams(collective_id=0, has_side_effects=True, vmem_limit_bytes=60 * 2**20),
        name="panel_factor",
    )(panel_index, tiles, diag)


def direct(root_matrix, inverse_block, link_tiles, tile_mask, panel_index):
    row_block, col_block = root_matrix.shape
    tiles, diag = scenario_tiles(root_matrix, inverse_block[0], link_tiles[0], tile_mask, panel_index)
    factor_rows, own_rows, own_cols = panel_factor(panel_index, tiles, diag, row_block, col_block)
    update = lax.dot_general(
        own_rows, own_cols, (((1,), (1,)), ((), ())), preferred_element_type=jnp.float32
    )
    return (root_matrix - update, factor_rows)


def solution(mesh):
    in_specs = (
        P(("scen", "row"), "col"),
        P(("scen", "row", "col"), None, None),
        P(("scen", "row", "col"), None, None, None),
        P(("scen", "row", "col"), None),
        P(),
    )
    out_specs = (P(("scen", "row"), "col"), P(("scen", "row", "col"), None))
    sizes = tuple(mesh.shape[a] for a in ("scen", "row", "col"))
    body = direct if sizes == (2, 4, 4) else local
    return jax.shard_map(body, mesh=mesh, in_specs=in_specs, out_specs=out_specs, check_vma=False)
```

```python
import jax
import jax.numpy as jnp
from jax import lax
from jax.experimental import pallas as pl
from jax.experimental.pallas import tpu as pltpu
from jax.sharding import PartitionSpec as P

PANEL = 128


def broadcast(block, axis, source):
    block = jnp.where(lax.axis_index(axis) == source, block, jnp.zeros_like(block))
    return lax.psum(block, axis)


def select_matrix(tile_flags, slot_count):
    slot_order = jnp.cumsum(tile_flags) - 1
    slot_ids = lax.broadcasted_iota(jnp.int32, (slot_count, tile_flags.shape[0]), 0)
    hit = (slot_order[None, :] == slot_ids) & (tile_flags[None, :] == 1)
    return jnp.where(hit, jnp.float32(1.0), jnp.float32(0.0))


def compact_term(inverse, tiles_here, tile_flags, panel_at):
    slot_count, inner_rows, tile_rows = tiles_here.shape
    selector = select_matrix(tile_flags, slot_count)
    per_panel = PANEL // tile_rows
    picked = lax.dynamic_slice_in_dim(selector, panel_at * per_panel, per_panel, 1)
    columns = jnp.einsum(
        "kj,knt->njt", picked.astype(jnp.bfloat16), tiles_here, preferred_element_type=jnp.float32
    )
    columns = columns.reshape(inner_rows, PANEL).astype(jnp.bfloat16)
    weighted = jnp.dot(inverse, columns, preferred_element_type=jnp.float32).astype(jnp.bfloat16)
    product = jnp.einsum("knt,na->kta", tiles_here, weighted, preferred_element_type=jnp.float32)
    return (selector, product)


def dense_term(selector, product, base_cols, base_start):
    spread = jnp.einsum("kr,kta->rta", selector, product, precision=lax.Precision.HIGHEST)
    scenario = spread.reshape(selector.shape[1] * product.shape[1], PANEL)
    own_block = lax.dynamic_slice_in_dim(scenario, base_start, base_cols.shape[0], 0) + base_cols
    return lax.dynamic_update_slice_in_dim(scenario, own_block, base_start, 0)


def lower_rows(diagonal, rows_here, first_row, first_col):
    chol_lower = jnp.linalg.cholesky(diagonal)
    solved = jax.scipy.linalg.solve_triangular(chol_lower, rows_here.T, lower=True).T
    row_ids = first_row + lax.broadcasted_iota(jnp.int32, (rows_here.shape[0], 1), 0)
    return jnp.where(row_ids >= first_col, solved, 0.0)


def trailing_rows(factor_part, first_row, first_col):
    rounded = factor_part.astype(jnp.bfloat16)
    row_ids = first_row + lax.broadcasted_iota(jnp.int32, (factor_part.shape[0], 1), 0)
    return jnp.where(row_ids >= first_col + PANEL, rounded, jnp.zeros_like(rounded))


def local(root_matrix, inverse_block, link_tiles, tile_mask, panel_index):
    panel_at = panel_index[0]
    tile_flags = tile_mask[0]
    selector, product = compact_term(inverse_block[0], link_tiles[0], tile_flags, panel_at)
    tile_count = selector.shape[1]
    tile_rows = product.shape[1]
    total_rows = tile_count * tile_rows
    row_block, col_block = root_matrix.shape
    scen_at = lax.axis_index("scen")
    row_at = lax.axis_index("row")
    col_at = lax.axis_index("col")
    row_count = lax.axis_size("row")
    col_count = lax.axis_size("col")
    scen_count = lax.axis_size("scen")
    block_at = scen_at * row_count + row_at
    first_col = panel_at * PANEL
    owner_col = first_col // col_block
    base_cols = lax.dynamic_slice_in_dim(root_matrix, first_col - owner_col * col_block, PANEL, 1)
    base_cols = jnp.where(col_at == owner_col, base_cols, 0.0)
    piece_rows = row_block // col_count
    scenario = dense_term(selector, product, base_cols, block_at * row_block)
    slab_rows = total_rows // scen_count
    slab_sum = lax.psum_scatter(scenario, "scen", scatter_dimension=0, tiled=True)
    slab_sum = lax.psum(slab_sum, ("row", "col"))
    owner_slab = first_col // slab_rows
    diag_part = lax.dynamic_slice_in_dim(slab_sum, first_col - owner_slab * slab_rows, PANEL, 0)
    diagonal = broadcast(diag_part, "scen", owner_slab)
    slab_first = scen_at * slab_rows
    slab_factor = lower_rows(diagonal, slab_sum, slab_first, first_col)
    factor_rows = lax.dynamic_slice_in_dim(
        slab_factor, (row_at * col_count + col_at) * piece_rows, piece_rows, 0
    )
    ending = trailing_rows(slab_factor, slab_first, first_col)
    all_factor = lax.all_gather(ending, "scen", axis=0, tiled=True)
    own_rows = lax.dynamic_slice_in_dim(all_factor, block_at * row_block, row_block, 0)
    own_cols = lax.dynamic_slice_in_dim(all_factor, col_at * col_block, col_block, 0)
    update = lax.dot_general(
        own_rows, own_cols, (((1,), (1,)), ((), ())), preferred_element_type=jnp.float32
    )
    return (root_matrix - update, factor_rows)


MESH_ID = pl.DeviceIdType.MESH
F32 = jnp.float32
BF16 = jnp.bfloat16


def term_kernel(panel_ref, mask_ref, inv_hbm, tiles_hbm, root_ref, out_ref, diag_ref, inv, tiles, left, sems):
    slots = tiles.shape[0]
    f = panel_ref[0]
    scen_at, row_at, col_at = (lax.axis_index(a) for a in ("scen", "row", "col"))
    group = scen_at * lax.axis_size("row") + row_at
    inv_copy = pltpu.make_async_copy(inv_hbm, inv, sems.at[slots])
    inv_copy.start()

    def tile_copy(k):
        return pltpu.make_async_copy(tiles_hbm.at[k], tiles.at[k], sems.at[k])

    tile_total = mask_ref.shape[1]
    before = lax.fori_loop(0, f, lambda t, n: n + mask_ref[0, t], 0)
    total = lax.fori_loop(f, tile_total, lambda t, n: n + mask_ref[0, t], before)
    linked = mask_ref[0, f]
    first = jnp.minimum(before, slots - 1)
    panel_copy = pltpu.make_async_copy(tiles_hbm.at[first], left, sems.at[slots + 1])
    panel_copy.start()

    @pl.loop(0, total)
    def _(k):
        tile_copy(k).start()

    panel_copy.wait()
    columns = jnp.where(linked == 1, left[...], jnp.zeros_like(left))
    inv_copy.wait()
    weighted = lax.dot_general(
        columns, inv[...], (((0,), (0,)), ((), ())), preferred_element_type=F32
    ).astype(BF16)

    def one(t, at):
        flag = mask_ref[0, t]

        @pl.when(flag == 1)
        def _():
            tile_copy(at).wait()
            out_ref[t] = jnp.dot(weighted, tiles[at], preferred_element_type=F32)

        @pl.when(flag != 1)
        def _():
            out_ref[t] = jnp.zeros(out_ref.shape[1:], F32)

        return at + flag

    lax.fori_loop(0, tile_total, one, 0)
    own_tiles = root_ref.shape[0] // PANEL

    @pl.when(col_at == f // (tile_total // lax.axis_size("col")))
    def _():
        for i in range(own_tiles):
            at = group * own_tiles + i
            out_ref[at] = out_ref[at] + root_ref[i * PANEL : (i + 1) * PANEL, :].T

    diag_ref[...] = out_ref[f]


def scenario_tiles(root_matrix, inverse, tiles, tile_mask, panel_index):
    slots, inner, tile_rows = tiles.shape
    tile_total = tile_mask.shape[1]
    own_rows, own_cols = root_matrix.shape
    wide = own_cols // PANEL
    return pl.pallas_call(
        term_kernel,
        out_shape=(
            jax.ShapeDtypeStruct((tile_total, PANEL, tile_rows), F32),
            jax.ShapeDtypeStruct((PANEL, PANEL), F32),
        ),
        grid_spec=pltpu.PrefetchScalarGridSpec(
            num_scalar_prefetch=2,
            grid=(1,),
            in_specs=[
                pl.BlockSpec(memory_space=pltpu.HBM),
                pl.BlockSpec(memory_space=pltpu.HBM),
                pl.BlockSpec((own_rows, PANEL), lambda i, p, m: (0, lax.rem(p[0], wide))),
            ],
            out_specs=[
                pl.BlockSpec((tile_total, PANEL, tile_rows), lambda i, p, m: (0, 0, 0)),
                pl.BlockSpec((PANEL, PANEL), lambda i, p, m: (0, 0)),
            ],
            scratch_shapes=[
                pltpu.VMEM(inverse.shape, BF16),
                pltpu.VMEM(tiles.shape, BF16),
                pltpu.VMEM((inner, tile_rows), BF16),
                pltpu.SemaphoreType.DMA((slots + 2,)),
            ],
        ),
        compiler_params=pltpu.CompilerParams(vmem_limit_bytes=60 * 2**20),
        name="scenario_tiles",
    )(panel_index, tile_mask, inverse, tiles, root_matrix)


def remote(src, dst, send, recv, device):
    return pltpu.make_async_remote_copy(
        src_ref=src, dst_ref=dst, send_sem=send, recv_sem=recv, device_id=device, device_id_type=MESH_ID
    )


def invert_blocks(state, inv_ref, start, stop):
    lane = lax.broadcasted_iota(jnp.int32, (8, PANEL), 1)
    sub = lax.broadcasted_iota(jnp.int32, (8, 1), 0)

    def block(b, carry):
        at = pl.ds(pl.multiple_of(b * 8, 8), 8)
        strip = state[at, :]
        for i in range(8):
            col = jnp.sum(jnp.where(lane == b * 8 + i, strip[:, :PANEL], 0.0), axis=1, keepdims=True)
            pivot = col[i : i + 1, :]
            inv = lax.rsqrt(pivot)
            inv = inv * (1.5 - 0.5 * pivot * inv * inv)
            row = strip[i : i + 1, :] * inv
            coef = jnp.where(sub > i, col * inv, 0.0)
            strip = jnp.where(sub == i, row, strip - coef * row)
        inv_ref[at, :] = strip[:, PANEL:]
        later = jnp.where(lane >= b * 8 + 8, strip[:, :PANEL], 0.0)
        state[...] = state[...] - lax.dot_general(
            later, strip, (((0,), (0,)), ((), ())), preferred_element_type=F32, precision=lax.Precision.HIGHEST
        )
        return carry

    lax.fori_loop(start, stop, block, 0)


def gather_phase(panel_ref, piece_ref, inv_ref, factor_ref, rows_ref, cols_ref, send_z, recv_z,
                 send_x, send_y, recv_p, send_c, recv_c):
    s, r, c = (lax.axis_index(a) for a in ("scen", "row", "col"))
    y, k = r // 2, lax.rem(r, 2)
    rows = factor_ref.shape[0]
    far_x = lax.rem(s + c // 2, 2)
    far_y = lax.rem(y + c, 2)
    source = jnp.logical_and(far_x == 0, far_y == 0)
    x_to = (1 - s, r, c)
    y_to = (s, 2 * (1 - y) + k, c)
    core = (s, 2 * y + 1 - k, c)

    def row_at(z):
        return rows_ref.at[pl.ds(pl.multiple_of(z * rows, rows), rows)]

    def col_at(kk, z):
        return cols_ref.at[pl.ds(pl.multiple_of((kk * 4 + z) * rows, rows), rows)]

    f = panel_ref[0]
    first = (s * 4 + r) * (4 * rows) + c * rows
    for i in range(2):
        part = lax.dot_general(
            piece_ref[i], inv_ref[...], (((0,), (1,)), ((), ())),
            preferred_element_type=F32, precision=lax.Precision.HIGHEST,
        )
        ids = first + i * PANEL + lax.broadcasted_iota(jnp.int32, part.shape, 0)
        factor_ref[i * PANEL : (i + 1) * PANEL, :] = jnp.where(ids >= f * PANEL, part, 0.0)
        ending = jnp.where(ids >= f * PANEL + PANEL, part, 0.0).astype(BF16)
        rows_ref[pl.ds(pl.multiple_of(c * rows + i * PANEL, PANEL), PANEL), :] = ending

    z_copies = []
    for o in range(1, 4):
        cp = remote(row_at(c), row_at(c), send_z.at[o - 1], recv_z.at[o - 1], (s, r, lax.rem(c + o, 4)))
        cp.start()
        z_copies.append(cp)

    def z_arrival(o):
        remote(row_at(lax.rem(c + 4 - o, 4)), row_at(lax.rem(c + 4 - o, 4)), send_z.at[o - 1], recv_z.at[o - 1], core).wait_recv()

    for o in range(4):
        z = lax.rem(c + 4 - o, 4)
        here = col_at(k, z)
        to_x = remote(here, here, send_x.at[o], recv_p.at[o], x_to)
        to_y = remote(here, here, send_y.at[o], recv_p.at[o], y_to)

        @pl.when(source)
        def _():
            if o:
                z_arrival(o)
            here[...] = row_at(z)[...]
            to_x.start()
            to_y.start()

        @pl.when(jnp.logical_not(source))
        def _():
            to_x.wait_recv()

        @pl.when(jnp.logical_and(far_x == 1, far_y == 0) if o < 2 else jnp.logical_and(far_x == 0, far_y == 1))
        def _():
            (to_y if o < 2 else to_x).start()

        remote(here, here, send_c.at[o], recv_c.at[o], core).start()

    @pl.when(jnp.logical_not(source))
    def _():
        for o in range(1, 4):
            z_arrival(o)

    for o in range(4):
        z = lax.rem(c + 4 - o, 4)
        there, here = col_at(1 - k, z), col_at(k, z)
        remote(there, there, send_c.at[o], recv_c.at[o], core).wait_recv()
        remote(here, here, send_c.at[o], recv_c.at[o], core).wait_send()
        to_x = remote(here, here, send_x.at[o], recv_p.at[o], x_to)
        to_y = remote(here, here, send_y.at[o], recv_p.at[o], y_to)

        @pl.when(source)
        def _():
            to_x.wait_send()
            to_y.wait_send()

        @pl.when(jnp.logical_and(far_x == 1, far_y == 0) if o < 2 else jnp.logical_and(far_x == 0, far_y == 1))
        def _():
            (to_y if o < 2 else to_x).wait_send()

    for cp in z_copies:
        cp.wait_send()


def panel_kernel(panel_ref, tiles_hbm, diag_in, factor_ref, rows_ref, cols_ref, own, got0, got1, got2, onward, acc, got3, got4, final,
                 dsum, dgot, dpart, dparts, diag_ref, state, inv_ref, piece_ref, send, recv, local_sem, dsend, drecv,
                 *gather_sems):
    s, r, c = (lax.axis_index(a) for a in ("scen", "row", "col"))
    y, k = r // 2, lax.rem(r, 2)
    core = (s, 2 * y + 1 - k, c)
    x_to = (1 - s, r, c)
    y_to = (s, 2 * (1 - y) + k, c)
    z1 = c + 1 - 2 * lax.rem(c, 2)
    z2 = lax.rem(c + 2, 4)
    me = s * 8 + y * 4 + c

    def chip(o):
        q = lax.rem(me + o, 16)
        return q, (q // 8, 2 * lax.rem(q // 4, 2) + k, lax.rem(q, 4))

    barrier = pltpu.get_barrier_semaphore()
    pl.semaphore_signal(barrier, inc=1, device_id=core, device_id_type=MESH_ID)
    for o in range(1, 16):
        pl.semaphore_signal(barrier, inc=1, device_id=chip(o)[1], device_id_type=MESH_ID)
    pl.semaphore_wait(barrier, 16)

    core_diag = remote(diag_in, dgot, dsend.at[0], drecv.at[0], core)
    core_diag.start()
    far = (1 - s) * 2 + 1 - y
    over_x = (1 - s) * 2 + y
    over_y = s * 2 + 1 - y
    here = s * 2 + y
    par = lax.rem(c, 2)
    hi = c // 2
    order = (far, over_x, over_y, here)
    core_copy = []
    loads = []
    for n, i in enumerate(order):
        theirs = pl.ds(pl.multiple_of((i * 2 + 1 - k) * 8, 8), 8)
        ours = pl.ds(pl.multiple_of((i * 2 + k) * 8, 8), 8)
        cp = remote(tiles_hbm.at[theirs], got0.at[n], send.at[n], recv.at[n], core)
        cp.start()
        core_copy.append(cp)
        ld = pltpu.make_async_copy(tiles_hbm.at[ours], own.at[n], local_sem.at[n])
        ld.start()
        loads.append(ld)
    core_diag.wait()
    dsum[...] = diag_in[...] + dgot[...]
    out1 = []
    for o in range(1, 16):
        q, dev = chip(o)
        cp = remote(dsum.at[pl.ds(pl.multiple_of(q * 8, 8), 8)], dparts.at[o], dsend.at[o], drecv.at[o], dev)
        cp.start()
        out1.append(cp)

    pair = (2 * (1 - par), 2 * par)

    def crossing(j, h, step):
        n = 0 if step == 0 else 1 + h
        at = 4 + (j * 2 + h) * 2 + step
        return remote(own.at[n, pl.ds(4 * h + pair[j], 2)], got1.at[h, j, step], send.at[at], recv.at[at], y_to if h else x_to)

    first = [[[crossing(j, h, step) for step in range(2)] for h in range(2)] for j in range(2)]

    def pair_sum(n):
        loads[n].wait()
        core_copy[n].wait_recv()
        own[n] = own[n] + got0[n]

    pair_sum(0)
    first[0][0][0].start()
    first[0][1][0].start()
    pair_sum(1)
    first[0][0][1].start()
    pair_sum(2)
    first[0][1][1].start()
    pair_sum(3)
    for cp in out1:
        cp.wait_recv()
    total = dsum[pl.ds(pl.multiple_of(me * 8, 8), 8), :]
    for o in range(1, 16):
        total = total + dparts[o]
    dpart[...] = total
    diag_ref[pl.ds(pl.multiple_of(me * 8, 8), 8), :] = total
    out2 = []
    for o in range(1, 16):
        q, dev = chip(o)
        cp = remote(dpart, diag_ref.at[pl.ds(pl.multiple_of(me * 8, 8), 8)], dsend.at[15 + o], drecv.at[15 + o], dev)
        cp.start()
        out2.append(cp)
    second = []
    for j in range(2):
        for h in range(2):
            first[j][h][0].wait_recv()
            onward[j, h] = own[2 - h, pl.ds(4 * h + pair[j], 2)] + got1[h, j, 0]
            at = 12 + j * 2 + h
            cp = remote(onward.at[j, h], got2.at[j, h], send.at[at], recv.at[at], x_to if h else y_to)
            cp.start()
            second.append(cp)
            if j == 0:
                first[1][h][0].start()
        if j == 0:
            for cp in out2:
                cp.wait_recv()
            full = diag_ref[...]
            state[:, :PANEL] = 0.5 * (full + full.T)
            state[:, PANEL:] = jnp.where(
                lax.broadcasted_iota(jnp.int32, (PANEL, PANEL), 0) == lax.broadcasted_iota(jnp.int32, (PANEL, PANEL), 1),
                1.0, 0.0,
            )
        invert_blocks(state, inv_ref, (0, 6)[j], (2, 9)[j])
        for h in range(2):
            first[j][h][1].wait_recv()
            acc[j, h] = own[3, pl.ds(4 * h + pair[j], 2)] + got1[h, j, 1]
            if j == 0:
                first[1][h][1].start()
        invert_blocks(state, inv_ref, (2, 9)[j], (4, 12)[j])
        for h in range(2):
            second[2 * j + h].wait_recv()
            acc[j, h] = acc[j, h] + got2[j, h]
        if j == 0:
            z_out = remote(acc.at[0], got3, send.at[16], recv.at[16], (s, r, z1))
            z_out.start()
            invert_blocks(state, inv_ref, 4, 6)
    z_out.wait_recv()
    final[...] = acc[1, 1 - hi] + got3[1 - hi]
    last = remote(final, got4, send.at[17], recv.at[17], (s, r, z2))
    last.start()
    mine = acc[1, hi] + got3[hi]
    invert_blocks(state, inv_ref, 12, 16)
    last.wait_recv()
    piece_ref[...] = mine + got4[...]
    for cp in core_copy + out1 + out2 + second + [z_out, last]:
        cp.wait_send()
    for j in range(2):
        for h in range(2):
            for step in range(2):
                first[j][h][step].wait_send()
    gather_phase(panel_ref, piece_ref, inv_ref, factor_ref, rows_ref, cols_ref, *gather_sems)


def panel_factor(panel_index, tiles, diag, row_block, col_block):
    tile = tiles.shape[1:]
    vmem = pl.BlockSpec(memory_space=pltpu.VMEM)
    return pl.pallas_call(
        panel_kernel,
        out_shape=(
            jax.ShapeDtypeStruct((2 * PANEL, PANEL), F32),
            jax.ShapeDtypeStruct((row_block, PANEL), BF16),
            jax.ShapeDtypeStruct((col_block, PANEL), BF16),
        ),
        in_specs=[pl.BlockSpec(memory_space=pltpu.SMEM), pl.BlockSpec(memory_space=pl.ANY), vmem],
        out_specs=(vmem, vmem, vmem),
        scratch_shapes=[
            pltpu.VMEM((4, 8, *tile), F32),
            pltpu.VMEM((4, 8, *tile), F32),
            pltpu.VMEM((2, 2, 2, 2, *tile), F32),
            pltpu.VMEM((2, 2, 2, *tile), F32),
            pltpu.VMEM((2, 2, 2, *tile), F32),
            pltpu.VMEM((2, 2, 2, *tile), F32),
            pltpu.VMEM((2, 2, *tile), F32),
            pltpu.VMEM((2, *tile), F32),
            pltpu.VMEM((2, *tile), F32),
            pltpu.VMEM(tile, F32),
            pltpu.VMEM(tile, F32),
            pltpu.VMEM((8, PANEL), F32),
            pltpu.VMEM((16, 8, PANEL), F32),
            pltpu.VMEM(tile, F32),
            pltpu.VMEM((PANEL, 2 * PANEL), F32),
            pltpu.VMEM(tile, F32),
            pltpu.VMEM((2, *tile), F32),
            pltpu.SemaphoreType.DMA((18,)),
            pltpu.SemaphoreType.DMA((18,)),
            pltpu.SemaphoreType.DMA((4,)),
            pltpu.SemaphoreType.DMA((31,)),
            pltpu.SemaphoreType.DMA((31,)),
            pltpu.SemaphoreType.DMA((3,)),
            pltpu.SemaphoreType.DMA((3,)),
            *[pltpu.SemaphoreType.DMA((4,))] * 5,
        ],
        compiler_params=pltpu.CompilerParams(collective_id=0, has_side_effects=True, vmem_limit_bytes=60 * 2**20),
        name="panel_factor",
    )(panel_index, tiles, diag)


def direct(root_matrix, inverse_block, link_tiles, tile_mask, panel_index):
    row_block, col_block = root_matrix.shape
    tiles, diag = scenario_tiles(root_matrix, inverse_block[0], link_tiles[0], tile_mask, panel_index)
    factor_rows, own_rows, own_cols = panel_factor(panel_index, tiles, diag, row_block, col_block)
    update = lax.dot_general(
        own_rows, own_cols, (((1,), (1,)), ((), ())), preferred_element_type=jnp.float32
    )
    return (root_matrix - update, factor_rows)


def solution(mesh):
    in_specs = (
        P(("scen", "row"), "col"),
        P(("scen", "row", "col"), None, None),
        P(("scen", "row", "col"), None, None, None),
        P(("scen", "row", "col"), None),
        P(),
    )
    out_specs = (P(("scen", "row"), "col"), P(("scen", "row", "col"), None))
    sizes = tuple(mesh.shape[a] for a in ("scen", "row", "col"))
    body = direct if sizes == (2, 4, 4) else local
    return jax.shard_map(body, mesh=mesh, in_specs=in_specs, out_specs=out_specs, check_vma=False)
```

```python
import jax
import jax.numpy as jnp
from jax import lax
from jax.experimental import pallas as pl
from jax.experimental.pallas import tpu as pltpu
from jax.sharding import PartitionSpec as P

PANEL = 128


def broadcast(block, axis, source):
    block = jnp.where(lax.axis_index(axis) == source, block, jnp.zeros_like(block))
    return lax.psum(block, axis)


def select_matrix(tile_flags, slot_count):
    slot_order = jnp.cumsum(tile_flags) - 1
    slot_ids = lax.broadcasted_iota(jnp.int32, (slot_count, tile_flags.shape[0]), 0)
    hit = (slot_order[None, :] == slot_ids) & (tile_flags[None, :] == 1)
    return jnp.where(hit, jnp.float32(1.0), jnp.float32(0.0))


def compact_term(inverse, tiles_here, tile_flags, panel_at):
    slot_count, inner_rows, tile_rows = tiles_here.shape
    selector = select_matrix(tile_flags, slot_count)
    per_panel = PANEL // tile_rows
    picked = lax.dynamic_slice_in_dim(selector, panel_at * per_panel, per_panel, 1)
    columns = jnp.einsum(
        "kj,knt->njt", picked.astype(jnp.bfloat16), tiles_here, preferred_element_type=jnp.float32
    )
    columns = columns.reshape(inner_rows, PANEL).astype(jnp.bfloat16)
    weighted = jnp.dot(inverse, columns, preferred_element_type=jnp.float32).astype(jnp.bfloat16)
    product = jnp.einsum("knt,na->kta", tiles_here, weighted, preferred_element_type=jnp.float32)
    return (selector, product)


def dense_term(selector, product, base_cols, base_start):
    spread = jnp.einsum("kr,kta->rta", selector, product, precision=lax.Precision.HIGHEST)
    scenario = spread.reshape(selector.shape[1] * product.shape[1], PANEL)
    own_block = lax.dynamic_slice_in_dim(scenario, base_start, base_cols.shape[0], 0) + base_cols
    return lax.dynamic_update_slice_in_dim(scenario, own_block, base_start, 0)


def lower_rows(diagonal, rows_here, first_row, first_col):
    chol_lower = jnp.linalg.cholesky(diagonal)
    solved = jax.scipy.linalg.solve_triangular(chol_lower, rows_here.T, lower=True).T
    row_ids = first_row + lax.broadcasted_iota(jnp.int32, (rows_here.shape[0], 1), 0)
    return jnp.where(row_ids >= first_col, solved, 0.0)


def trailing_rows(factor_part, first_row, first_col):
    rounded = factor_part.astype(jnp.bfloat16)
    row_ids = first_row + lax.broadcasted_iota(jnp.int32, (factor_part.shape[0], 1), 0)
    return jnp.where(row_ids >= first_col + PANEL, rounded, jnp.zeros_like(rounded))


def local(root_matrix, inverse_block, link_tiles, tile_mask, panel_index):
    panel_at = panel_index[0]
    tile_flags = tile_mask[0]
    selector, product = compact_term(inverse_block[0], link_tiles[0], tile_flags, panel_at)
    tile_count = selector.shape[1]
    tile_rows = product.shape[1]
    total_rows = tile_count * tile_rows
    row_block, col_block = root_matrix.shape
    scen_at = lax.axis_index("scen")
    row_at = lax.axis_index("row")
    col_at = lax.axis_index("col")
    row_count = lax.axis_size("row")
    col_count = lax.axis_size("col")
    scen_count = lax.axis_size("scen")
    block_at = scen_at * row_count + row_at
    first_col = panel_at * PANEL
    owner_col = first_col // col_block
    base_cols = lax.dynamic_slice_in_dim(root_matrix, first_col - owner_col * col_block, PANEL, 1)
    base_cols = jnp.where(col_at == owner_col, base_cols, 0.0)
    piece_rows = row_block // col_count
    scenario = dense_term(selector, product, base_cols, block_at * row_block)
    slab_rows = total_rows // scen_count
    slab_sum = lax.psum_scatter(scenario, "scen", scatter_dimension=0, tiled=True)
    slab_sum = lax.psum(slab_sum, ("row", "col"))
    owner_slab = first_col // slab_rows
    diag_part = lax.dynamic_slice_in_dim(slab_sum, first_col - owner_slab * slab_rows, PANEL, 0)
    diagonal = broadcast(diag_part, "scen", owner_slab)
    slab_first = scen_at * slab_rows
    slab_factor = lower_rows(diagonal, slab_sum, slab_first, first_col)
    factor_rows = lax.dynamic_slice_in_dim(
        slab_factor, (row_at * col_count + col_at) * piece_rows, piece_rows, 0
    )
    ending = trailing_rows(slab_factor, slab_first, first_col)
    all_factor = lax.all_gather(ending, "scen", axis=0, tiled=True)
    own_rows = lax.dynamic_slice_in_dim(all_factor, block_at * row_block, row_block, 0)
    own_cols = lax.dynamic_slice_in_dim(all_factor, col_at * col_block, col_block, 0)
    update = lax.dot_general(
        own_rows, own_cols, (((1,), (1,)), ((), ())), preferred_element_type=jnp.float32
    )
    return (root_matrix - update, factor_rows)


MESH_ID = pl.DeviceIdType.MESH
F32 = jnp.float32
BF16 = jnp.bfloat16


def term_kernel(panel_ref, mask_ref, inv_hbm, tiles_hbm, root_ref, out_ref, diag_ref, inv, tiles, left, sems):
    slots = tiles.shape[0]
    f = panel_ref[0]
    scen_at, row_at, col_at = (lax.axis_index(a) for a in ("scen", "row", "col"))
    group = scen_at * lax.axis_size("row") + row_at
    inv_copy = pltpu.make_async_copy(inv_hbm, inv, sems.at[slots])
    inv_copy.start()

    def tile_copy(k):
        return pltpu.make_async_copy(tiles_hbm.at[k], tiles.at[k], sems.at[k])

    tile_total = mask_ref.shape[1]
    before = lax.fori_loop(0, f, lambda t, n: n + mask_ref[0, t], 0)
    total = lax.fori_loop(f, tile_total, lambda t, n: n + mask_ref[0, t], before)
    linked = mask_ref[0, f]
    first = jnp.minimum(before, slots - 1)
    panel_copy = pltpu.make_async_copy(tiles_hbm.at[first], left, sems.at[slots + 1])
    panel_copy.start()

    @pl.loop(0, total)
    def _(k):
        tile_copy(k).start()

    panel_copy.wait()
    columns = jnp.where(linked == 1, left[...], jnp.zeros_like(left))
    inv_copy.wait()
    weighted = lax.dot_general(
        columns, inv[...], (((0,), (0,)), ((), ())), preferred_element_type=F32
    ).astype(BF16)

    def one(t, at):
        flag = mask_ref[0, t]

        @pl.when(flag == 1)
        def _():
            tile_copy(at).wait()
            out_ref[t] = jnp.dot(weighted, tiles[at], preferred_element_type=F32)

        @pl.when(flag != 1)
        def _():
            out_ref[t] = jnp.zeros(out_ref.shape[1:], F32)

        return at + flag

    lax.fori_loop(0, tile_total, one, 0)
    own_tiles = root_ref.shape[0] // PANEL

    @pl.when(col_at == f // (tile_total // lax.axis_size("col")))
    def _():
        for i in range(own_tiles):
            at = group * own_tiles + i
            out_ref[at] = out_ref[at] + root_ref[i * PANEL : (i + 1) * PANEL, :].T

    diag_ref[...] = out_ref[f]


def scenario_tiles(root_matrix, inverse, tiles, tile_mask, panel_index):
    slots, inner, tile_rows = tiles.shape
    tile_total = tile_mask.shape[1]
    own_rows, own_cols = root_matrix.shape
    wide = own_cols // PANEL
    return pl.pallas_call(
        term_kernel,
        out_shape=(
            jax.ShapeDtypeStruct((tile_total, PANEL, tile_rows), F32),
            jax.ShapeDtypeStruct((PANEL, PANEL), F32),
        ),
        grid_spec=pltpu.PrefetchScalarGridSpec(
            num_scalar_prefetch=2,
            grid=(1,),
            in_specs=[
                pl.BlockSpec(memory_space=pltpu.HBM),
                pl.BlockSpec(memory_space=pltpu.HBM),
                pl.BlockSpec((own_rows, PANEL), lambda i, p, m: (0, lax.rem(p[0], wide))),
            ],
            out_specs=[
                pl.BlockSpec((tile_total, PANEL, tile_rows), lambda i, p, m: (0, 0, 0)),
                pl.BlockSpec((PANEL, PANEL), lambda i, p, m: (0, 0)),
            ],
            scratch_shapes=[
                pltpu.VMEM(inverse.shape, BF16),
                pltpu.VMEM(tiles.shape, BF16),
                pltpu.VMEM((inner, tile_rows), BF16),
                pltpu.SemaphoreType.DMA((slots + 2,)),
            ],
        ),
        compiler_params=pltpu.CompilerParams(vmem_limit_bytes=60 * 2**20),
        name="scenario_tiles",
    )(panel_index, tile_mask, inverse, tiles, root_matrix)


def remote(src, dst, send, recv, device):
    return pltpu.make_async_remote_copy(
        src_ref=src, dst_ref=dst, send_sem=send, recv_sem=recv, device_id=device, device_id_type=MESH_ID
    )


def invert_blocks(state, inv_ref, start, stop):
    lane = lax.broadcasted_iota(jnp.int32, (8, PANEL), 1)
    sub = lax.broadcasted_iota(jnp.int32, (8, 1), 0)

    def block(b, carry):
        at = pl.ds(pl.multiple_of(b * 8, 8), 8)
        strip = state[at, :]
        for i in range(8):
            col = jnp.sum(jnp.where(lane == b * 8 + i, strip[:, :PANEL], 0.0), axis=1, keepdims=True)
            pivot = col[i : i + 1, :]
            inv = lax.rsqrt(pivot)
            inv = inv * (1.5 - 0.5 * pivot * inv * inv)
            row = strip[i : i + 1, :] * inv
            coef = jnp.where(sub > i, col * inv, 0.0)
            strip = jnp.where(sub == i, row, strip - coef * row)
        inv_ref[at, :] = strip[:, PANEL:]
        later = jnp.where(lane >= b * 8 + 8, strip[:, :PANEL], 0.0)
        state[...] = state[...] - lax.dot_general(
            later, strip, (((0,), (0,)), ((), ())), preferred_element_type=F32, precision=lax.Precision.HIGHEST
        )
        return carry

    lax.fori_loop(start, stop, block, 0)


def gather_phase(panel_ref, piece_ref, inv_ref, factor_ref, rows_ref, cols_ref, send_z, recv_z,
                 send_x, send_y, recv_p, send_c, recv_c):
    s, r, c = (lax.axis_index(a) for a in ("scen", "row", "col"))
    y, k = r // 2, lax.rem(r, 2)
    rows = factor_ref.shape[0]
    far_x = lax.rem(s + c // 2, 2)
    far_y = lax.rem(y + c, 2)
    source = jnp.logical_and(far_x == 0, far_y == 0)
    x_to = (1 - s, r, c)
    y_to = (s, 2 * (1 - y) + k, c)
    core = (s, 2 * y + 1 - k, c)

    def row_at(z):
        return rows_ref.at[pl.ds(pl.multiple_of(z * rows, rows), rows)]

    def col_at(kk, z):
        return cols_ref.at[pl.ds(pl.multiple_of((kk * 4 + z) * rows, rows), rows)]

    f = panel_ref[0]
    first = (s * 4 + r) * (4 * rows) + c * rows
    for i in range(2):
        part = lax.dot_general(
            piece_ref[i], inv_ref[...], (((0,), (1,)), ((), ())),
            preferred_element_type=F32, precision=lax.Precision.HIGHEST,
        )
        ids = first + i * PANEL + lax.broadcasted_iota(jnp.int32, part.shape, 0)
        factor_ref[i * PANEL : (i + 1) * PANEL, :] = jnp.where(ids >= f * PANEL, part, 0.0)
        ending = jnp.where(ids >= f * PANEL + PANEL, part, 0.0).astype(BF16)
        rows_ref[pl.ds(pl.multiple_of(c * rows + i * PANEL, PANEL), PANEL), :] = ending

    z_copies = []
    for o in range(1, 4):
        cp = remote(row_at(c), row_at(c), send_z.at[o - 1], recv_z.at[o - 1], (s, r, lax.rem(c + o, 4)))
        cp.start()
        z_copies.append(cp)

    def z_arrival(o):
        remote(row_at(lax.rem(c + 4 - o, 4)), row_at(lax.rem(c + 4 - o, 4)), send_z.at[o - 1], recv_z.at[o - 1], core).wait_recv()

    for o in range(4):
        z = lax.rem(c + 4 - o, 4)
        here = col_at(k, z)
        to_x = remote(here, here, send_x.at[o], recv_p.at[o], x_to)
        to_y = remote(here, here, send_y.at[o], recv_p.at[o], y_to)

        @pl.when(source)
        def _():
            if o:
                z_arrival(o)
            here[...] = row_at(z)[...]
            to_x.start()
            to_y.start()

        @pl.when(jnp.logical_not(source))
        def _():
            to_x.wait_recv()

        @pl.when(jnp.logical_and(far_x == 1, far_y == 0) if o < 2 else jnp.logical_and(far_x == 0, far_y == 1))
        def _():
            (to_y if o < 2 else to_x).start()

        remote(here, here, send_c.at[o], recv_c.at[o], core).start()

    @pl.when(jnp.logical_not(source))
    def _():
        for o in range(1, 4):
            z_arrival(o)

    for o in range(4):
        z = lax.rem(c + 4 - o, 4)
        there, here = col_at(1 - k, z), col_at(k, z)
        remote(there, there, send_c.at[o], recv_c.at[o], core).wait_recv()
        remote(here, here, send_c.at[o], recv_c.at[o], core).wait_send()
        to_x = remote(here, here, send_x.at[o], recv_p.at[o], x_to)
        to_y = remote(here, here, send_y.at[o], recv_p.at[o], y_to)

        @pl.when(source)
        def _():
            to_x.wait_send()
            to_y.wait_send()

        @pl.when(jnp.logical_and(far_x == 1, far_y == 0) if o < 2 else jnp.logical_and(far_x == 0, far_y == 1))
        def _():
            (to_y if o < 2 else to_x).wait_send()

    for cp in z_copies:
        cp.wait_send()


def panel_kernel(panel_ref, tiles_hbm, diag_in, factor_ref, rows_ref, cols_ref, own, got0, got1, got2, onward, acc, got3, got4, final,
                 dsum, dgot, dpart, dparts, diag_ref, state, inv_ref, piece_ref, send, recv, local_sem, dsend, drecv,
                 *gather_sems):
    s, r, c = (lax.axis_index(a) for a in ("scen", "row", "col"))
    y, k = r // 2, lax.rem(r, 2)
    core = (s, 2 * y + 1 - k, c)
    x_to = (1 - s, r, c)
    y_to = (s, 2 * (1 - y) + k, c)
    z1 = c + 1 - 2 * lax.rem(c, 2)
    z2 = lax.rem(c + 2, 4)
    me = s * 8 + y * 4 + c

    def chip(o):
        q = lax.rem(me + o, 16)
        return q, (q // 8, 2 * lax.rem(q // 4, 2) + k, lax.rem(q, 4))

    barrier = pltpu.get_barrier_semaphore()
    pl.semaphore_signal(barrier, inc=1, device_id=core, device_id_type=MESH_ID)
    for o in range(1, 16):
        pl.semaphore_signal(barrier, inc=1, device_id=chip(o)[1], device_id_type=MESH_ID)
    pl.semaphore_wait(barrier, 16)

    core_diag = remote(diag_in, dgot, dsend.at[0], drecv.at[0], core)
    core_diag.start()
    far = (1 - s) * 2 + 1 - y
    over_x = (1 - s) * 2 + y
    over_y = s * 2 + 1 - y
    here = s * 2 + y
    par = lax.rem(c, 2)
    hi = c // 2
    order = (far, over_x, over_y, here)
    core_copy = []
    loads = []
    for n, i in enumerate(order):
        theirs = pl.ds(pl.multiple_of((i * 2 + 1 - k) * 8, 8), 8)
        ours = pl.ds(pl.multiple_of((i * 2 + k) * 8, 8), 8)
        cp = remote(tiles_hbm.at[theirs], got0.at[n], send.at[n], recv.at[n], core)
        cp.start()
        core_copy.append(cp)
        ld = pltpu.make_async_copy(tiles_hbm.at[ours], own.at[n], local_sem.at[n])
        ld.start()
        loads.append(ld)
    core_diag.wait()
    dsum[...] = diag_in[...] + dgot[...]
    out1 = []
    for o in range(1, 16):
        q, dev = chip(o)
        cp = remote(dsum.at[pl.ds(pl.multiple_of(q * 8, 8), 8)], dparts.at[o], dsend.at[o], drecv.at[o], dev)
        cp.start()
        out1.append(cp)

    pair = (2 * (1 - par), 2 * par)

    def crossing(j, h, step):
        n = 0 if step == 0 else 1 + h
        at = 4 + (j * 2 + h) * 2 + step
        return remote(own.at[n, pl.ds(4 * h + pair[j], 2)], got1.at[h, j, step], send.at[at], recv.at[at], y_to if h else x_to)

    first = [[[crossing(j, h, step) for step in range(2)] for h in range(2)] for j in range(2)]

    def pair_sum(n):
        loads[n].wait()
        core_copy[n].wait_recv()
        own[n] = own[n] + got0[n]

    pair_sum(0)
    first[0][0][0].start()
    first[0][1][0].start()
    pair_sum(1)
    first[0][0][1].start()
    pair_sum(2)
    first[0][1][1].start()
    pair_sum(3)
    for cp in out1:
        cp.wait_recv()
    total = dsum[pl.ds(pl.multiple_of(me * 8, 8), 8), :]
    for o in range(1, 16):
        total = total + dparts[o]
    dpart[...] = total
    diag_ref[pl.ds(pl.multiple_of(me * 8, 8), 8), :] = total
    out2 = []
    for o in range(1, 16):
        q, dev = chip(o)
        cp = remote(dpart, diag_ref.at[pl.ds(pl.multiple_of(me * 8, 8), 8)], dsend.at[15 + o], drecv.at[15 + o], dev)
        cp.start()
        out2.append(cp)
    second = []
    for j in range(2):
        for h in range(2):
            first[j][h][0].wait_recv()
            onward[j, h] = own[2 - h, pl.ds(4 * h + pair[j], 2)] + got1[h, j, 0]
            at = 12 + j * 2 + h
            cp = remote(onward.at[j, h], got2.at[j, h], send.at[at], recv.at[at], x_to if h else y_to)
            cp.start()
            second.append(cp)
            if j == 0:
                first[1][h][0].start()
        if j == 0:
            for cp in out2:
                cp.wait_recv()
            full = diag_ref[...]
            state[:, :PANEL] = 0.5 * (full + full.T)
            state[:, PANEL:] = jnp.where(
                lax.broadcasted_iota(jnp.int32, (PANEL, PANEL), 0) == lax.broadcasted_iota(jnp.int32, (PANEL, PANEL), 1),
                1.0, 0.0,
            )
        invert_blocks(state, inv_ref, (0, 6)[j], (2, 9)[j])
        for h in range(2):
            first[j][h][1].wait_recv()
            acc[j, h] = own[3, pl.ds(4 * h + pair[j], 2)] + got1[h, j, 1]
            if j == 0:
                first[1][h][1].start()
        invert_blocks(state, inv_ref, (2, 9)[j], (4, 12)[j])
        for h in range(2):
            second[2 * j + h].wait_recv()
            acc[j, h] = acc[j, h] + got2[j, h]
        if j == 0:
            z_out = remote(acc.at[0], got3, send.at[16], recv.at[16], (s, r, z1))
            z_out.start()
            invert_blocks(state, inv_ref, 4, 6)
    z_out.wait_recv()
    final[...] = acc[1, 1 - hi] + got3[1 - hi]
    last = remote(final, got4, send.at[17], recv.at[17], (s, r, z2))
    last.start()
    mine = acc[1, hi] + got3[hi]
    invert_blocks(state, inv_ref, 12, 16)
    last.wait_recv()
    piece_ref[...] = mine + got4[...]
    for cp in core_copy + out1 + out2 + second + [z_out, last]:
        cp.wait_send()
    for j in range(2):
        for h in range(2):
            for step in range(2):
                first[j][h][step].wait_send()
    gather_phase(panel_ref, piece_ref, inv_ref, factor_ref, rows_ref, cols_ref, *gather_sems)


def panel_factor(panel_index, tiles, diag, row_block, col_block):
    tile = tiles.shape[1:]
    vmem = pl.BlockSpec(memory_space=pltpu.VMEM)
    return pl.pallas_call(
        panel_kernel,
        out_shape=(
            jax.ShapeDtypeStruct((2 * PANEL, PANEL), F32),
            jax.ShapeDtypeStruct((row_block, PANEL), BF16),
            jax.ShapeDtypeStruct((col_block, PANEL), BF16),
        ),
        in_specs=[pl.BlockSpec(memory_space=pltpu.SMEM), pl.BlockSpec(memory_space=pl.ANY), vmem],
        out_specs=(vmem, vmem, vmem),
        scratch_shapes=[
            pltpu.VMEM((4, 8, *tile), F32),
            pltpu.VMEM((4, 8, *tile), F32),
            pltpu.VMEM((2, 2, 2, 2, *tile), F32),
            pltpu.VMEM((2, 2, 2, *tile), F32),
            pltpu.VMEM((2, 2, 2, *tile), F32),
            pltpu.VMEM((2, 2, 2, *tile), F32),
            pltpu.VMEM((2, 2, *tile), F32),
            pltpu.VMEM((2, *tile), F32),
            pltpu.VMEM((2, *tile), F32),
            pltpu.VMEM(tile, F32),
            pltpu.VMEM(tile, F32),
            pltpu.VMEM((8, PANEL), F32),
            pltpu.VMEM((16, 8, PANEL), F32),
            pltpu.VMEM(tile, F32),
            pltpu.VMEM((PANEL, 2 * PANEL), F32),
            pltpu.VMEM(tile, F32),
            pltpu.VMEM((2, *tile), F32),
            pltpu.SemaphoreType.DMA((18,)),
            pltpu.SemaphoreType.DMA((18,)),
            pltpu.SemaphoreType.DMA((4,)),
            pltpu.SemaphoreType.DMA((31,)),
            pltpu.SemaphoreType.DMA((31,)),
            pltpu.SemaphoreType.DMA((3,)),
            pltpu.SemaphoreType.DMA((3,)),
            *[pltpu.SemaphoreType.DMA((4,))] * 5,
        ],
        compiler_params=pltpu.CompilerParams(collective_id=0, has_side_effects=True, vmem_limit_bytes=60 * 2**20),
        name="panel_factor",
    )(panel_index, tiles, diag)


def update_kernel(root_ref, rows_ref, cols_ref, out_ref):
    out_ref[...] = root_ref[...] - lax.dot_general(
        rows_ref[...], cols_ref[...], (((1,), (1,)), ((), ())), preferred_element_type=F32
    )


def trailing_update(root_matrix, own_rows, own_cols):
    row_block, col_block = root_matrix.shape
    step = PANEL
    return pl.pallas_call(
        update_kernel,
        out_shape=jax.ShapeDtypeStruct(root_matrix.shape, F32),
        grid=(row_block // step,),
        in_specs=[
            pl.BlockSpec((step, col_block), lambda i: (i, 0)),
            pl.BlockSpec((step, PANEL), lambda i: (i, 0)),
            pl.BlockSpec((col_block, PANEL), lambda i: (0, 0)),
        ],
        out_specs=pl.BlockSpec((step, col_block), lambda i: (i, 0)),
        compiler_params=pltpu.CompilerParams(vmem_limit_bytes=32 * 2**20),
        name="trailing_update",
    )(root_matrix, own_rows, own_cols)


def direct(root_matrix, inverse_block, link_tiles, tile_mask, panel_index):
    row_block, col_block = root_matrix.shape
    tiles, diag = scenario_tiles(root_matrix, inverse_block[0], link_tiles[0], tile_mask, panel_index)
    factor_rows, own_rows, own_cols = panel_factor(panel_index, tiles, diag, row_block, col_block)
    return (trailing_update(root_matrix, own_rows, own_cols), factor_rows)


def solution(mesh):
    in_specs = (
        P(("scen", "row"), "col"),
        P(("scen", "row", "col"), None, None),
        P(("scen", "row", "col"), None, None, None),
        P(("scen", "row", "col"), None),
        P(),
    )
    out_specs = (P(("scen", "row"), "col"), P(("scen", "row", "col"), None))
    sizes = tuple(mesh.shape[a] for a in ("scen", "row", "col"))
    body = direct if sizes == (2, 4, 4) else local
    return jax.shard_map(body, mesh=mesh, in_specs=in_specs, out_specs=out_specs, check_vma=False)
```
